32 devices in a mesh: loc: 16 (over z, x, core), yr: 2 (over y).
Axes of the slice: x: 2, y: 2, z: 4, core: 2. Of those that a mesh axis runs over, the one named last changes fastest.
Arguments:
- noise: bfloat16 [2, 111, 512, 1024], P(None, None, ('yr', 'loc')), parts along dimension 2, may hold values from -6 to 6
- loc_factor: bfloat16 [1024, 1024], P('loc'), as said below
- age_factor: bfloat16 [111, 111], replicated, as said below
- mean_rate: float32 [4, 111, 1024], P('yr'), parts along dimension 0, may hold values from -7 to -2
- population: float32 [4, 111, 1024], P('yr'), parts along dimension 0, may hold values from 0.1 to 10
- region_of: int32 [1024, 1], replicated, may hold values from 0 to 63
Outputs:
- log_rates: bfloat16 [2, 111, 1024, 512], P(None, None, 'loc', 'yr'), parts along dimension 3
- loc_survival: float32 [2, 1024, 512], P(None, 'loc', 'yr'), parts along dimension 2
- region_survival: float32 [2, 64, 512], P(None, 'loc', 'yr'), parts along dimension 2
The draws below stay inside these ranges and needn't reach their ends.
There are 2 independent parts, one for each index of `yr`. The reference program is written for one: setup_inputs(seed, part) draws one part's arguments, and reference() takes and returns one part's arrays. A program takes and returns all parts, laid end to end along the dimension named above; an argument that names none is the same for every part. Nothing has to cross between parts.
Inputs may be any that keep to these rules, and one draw needn't show every extreme that they name: `region_of`: every region holds at least one location. `loc_factor`: lower triangular with a positive diagonal. `age_factor`: lower triangular with a positive diagonal.
All inputs are finite; a program needn't handle non-finite values.
Results may differ from the reference program's by a relative error of at most 0.006.
Values may be sent and summed in bfloat16 or wider, within the bound.
No kernel may reach another device: no remote copies, remote signals or barrier semaphores. Data moves between devices by JAX's collectives and lax.ppermute only.
A program may use at most 128 MiB of HBM per device.

```python
import math
import jax
import jax.numpy as jnp
from jax import lax

SEXES = 2
AGES = 111
LOCS = 1024
REGIONS = 64
RD = 16
ROWS = 256
N_LOC = 16


def lower_factor(key, order, diag_lo, diag_hi, off_scale):
    first, second = jax.random.split(key)
    rows = lax.broadcasted_iota(jnp.int32, (order, order), 0)
    cols = lax.broadcasted_iota(jnp.int32, (order, order), 1)
    off = jax.random.normal(first, (order, order), jnp.float32) * off_scale / jnp.sqrt(rows.astype(jnp.float32) + 1.0)
    diag = jax.random.uniform(second, (order, order), jnp.float32, diag_lo, diag_hi)
    return jnp.where(cols < rows, off, jnp.where(cols == rows, diag, 0.0))


def draw_loc_factor(key, part):
    return lower_factor(key, LOCS, 0.7, 1.3, 0.5).astype(jnp.bfloat16)


def draw_age_factor(key, part):
    return lower_factor(key, AGES, 0.2, 0.4, 0.15).astype(jnp.bfloat16)


def block_levels(key, extent, cuts, least, top_value):
    loudness = 1.0
    for dim, parts in cuts:
        draws = jax.random.uniform(jax.random.fold_in(jax.random.fold_in(key, 6), dim), (parts,), jnp.float32, least / len(cuts), top_value / len(cuts))
        loudness = loudness * jnp.repeat(jnp.exp(draws), extent[dim] // parts).reshape((-1,) + (1,) * (len(extent) - 1 - dim))
    return loudness


def choose_distinct(stream_key, rows, count, top, lift):
    sequence = jax.random.permutation(jax.random.fold_in(stream_key, 1), count)
    favour = sequence
    for power in range(3):
        favour = favour * favour // count
    favour = favour * lift // count
    tickets = jax.random.randint(jax.random.fold_in(stream_key, 2), (rows, count), 0, 4096) + favour
    sure = jax.random.permutation(jax.random.fold_in(stream_key, 3), rows)[jnp.arange(count) % rows]
    tickets = jnp.where(jnp.arange(rows)[:, None] == sure[None, :], 1 << 14, tickets)
    score = tickets * count + jnp.arange(count)
    return lax.top_k(score.astype(jnp.int32), top)[1].astype(jnp.int32)


def gaussian(stream_key, dims, width, limit, cuts=(), kind=jnp.bfloat16):
    values = jax.random.normal(stream_key, dims, jnp.float32) * width
    if len(cuts) > 0:
        values = block_levels(stream_key, dims, cuts, -0.22, 0.18) * values
    return jnp.clip(values, min=-limit, max=limit).astype(kind)


def setup_inputs(seed: int = 0, part: int = 0) -> dict:
    streams_of = jax.random.split(jax.random.key(seed), 7)
    part_keys = jax.random.split(jax.random.fold_in(streams_of[6], part), 7)
    noise = gaussian(part_keys[0], (SEXES, AGES, ROWS, LOCS), 1.0, 6.0, ((2, 16),))
    loc_factor = draw_loc_factor(jax.random.fold_in(streams_of[6], 71), part)
    age_factor = draw_age_factor(jax.random.fold_in(streams_of[6], 71), part)
    mean_rate = jnp.clip(jax.random.uniform(part_keys[3], (SEXES, AGES, LOCS), jnp.float32, -7.0, -2.0), -7.0, -2.0)
    population = jnp.clip(jnp.exp(jax.random.uniform(part_keys[4], (SEXES, AGES, LOCS), jnp.float32, math.log(0.1), math.log(10.0))), 0.1, 10.0)
    region_of = choose_distinct(streams_of[5], LOCS, REGIONS, 1, 128)
    return {"noise": noise, "loc_factor": loc_factor, "age_factor": age_factor, "mean_rate": mean_rate, "population": population, "region_of": region_of}


def survival(rates):
    hazard = jnp.cumsum(rates, axis=1)
    after = jnp.exp(-hazard)
    total = 0.5 + jnp.sum(after, axis=1) - 0.5 * after[:, -1]
    return total / AGES


def reference(noise, loc_factor, age_factor, mean_rate, population, region_of):
    highest = lax.Precision.HIGHEST
    onehot = (region_of == jnp.arange(REGIONS, dtype=jnp.int32)[None, :]).astype(jnp.float32)
    totals = jnp.einsum('sal,lg->sag', population, onehot, precision=highest)
    blocks = jnp.moveaxis(noise.reshape(SEXES, AGES, N_LOC, RD, LOCS), 2, 0)
    loc_wide = loc_factor.astype(jnp.float32)
    age_wide = age_factor.astype(jnp.float32)

    def one_block(block):
        spread = jnp.einsum('sark,lk->sarl', block.astype(jnp.float32), loc_wide, precision=highest).astype(jnp.bfloat16)
        mixed = jnp.einsum('ab,sbrl->sarl', age_wide, spread.astype(jnp.float32), precision=highest)
        logs = (mean_rate[:, :, None, :] + mixed).astype(jnp.bfloat16)
        rates = jnp.exp(logs.astype(jnp.float32))
        weighted = jnp.einsum('sarl,lg->sarg', population[:, :, None, :] * rates, onehot, precision=highest)
        region_rates = weighted / totals[:, :, None, :]
        return logs, survival(rates), survival(region_rates)

    logs, loc_part, reg_part = lax.map(one_block, blocks)
    log_rates = jnp.transpose(logs, (1, 2, 4, 0, 3)).reshape(SEXES, AGES, LOCS, ROWS)
    loc_survival = jnp.transpose(loc_part, (1, 3, 0, 2)).reshape(SEXES, LOCS, ROWS)
    region_survival = jnp.transpose(reg_part, (1, 3, 0, 2)).reshape(SEXES, REGIONS, ROWS)
    return (log_rates, loc_survival, region_survival)
```

```python
import functools

import jax
import jax.numpy as jnp
from jax import lax
from jax.experimental import pallas as pl
from jax.experimental.pallas import tpu as pltpu
from jax.sharding import PartitionSpec as P

REGIONS = 64
LANES = 128
HALF = 64
NT = (((1,), (1,)), ((), ()))
CHUNKS = ((8, 12, 4, 0), (10, 14, 6, 2), (9, 13, 5, 1), (11, 15, 7, 3))


def survival(rates):
    hazard = jnp.cumsum(rates, axis=1)
    after = jnp.exp(-hazard)
    total = 0.5 + jnp.sum(after, axis=1) - 0.5 * after[:, -1]
    return total / rates.shape[1]


def shards_any(noise, loc_factor, age_factor, mean_rate, population, region_of):
    highest = lax.Precision.HIGHEST
    spread = jnp.einsum(
        "sark,lk->sarl",
        noise,
        lax.all_gather(loc_factor, "loc", axis=0, tiled=True),
        preferred_element_type=jnp.float32,
    ).astype(jnp.bfloat16)
    mixed = jnp.einsum("ab,sbrl->sarl", age_factor, spread, preferred_element_type=jnp.float32)
    log_section = (mean_rate[:, :, None, :] + mixed).astype(jnp.bfloat16)
    rates = jnp.exp(log_section.astype(jnp.float32))
    onehot = (region_of == jnp.arange(REGIONS, dtype=jnp.int32)[None, :]).astype(jnp.float32)
    totals = jnp.einsum("sal,lg->sag", population, onehot, precision=highest)
    weighted = jnp.einsum(
        "sarl,lg->sarg", population[:, :, None, :] * rates, onehot, precision=highest
    )
    region_section = survival(weighted / totals[:, :, None, :])
    region_moved = lax.all_to_all(region_section, "loc", split_axis=2, concat_axis=1, tiled=True)
    region_survival = jnp.transpose(region_moved, (0, 2, 1))
    turned = jnp.transpose(
        lax.all_to_all(log_section, "loc", split_axis=3, concat_axis=2, tiled=True), (0, 1, 3, 2)
    )
    loc_survival = survival(jnp.exp(turned.astype(jnp.float32)))
    return (turned, loc_survival, region_survival)


def split_bf16(x):
    hi = x.astype(jnp.bfloat16)
    return hi, (x - hi.astype(jnp.float32)).astype(jnp.bfloat16)


def age_mix_kernel(age_ref, x_ref, o_ref, wide_ref):
    ages = age_ref.shape[0]
    rows = x_ref.shape[1]
    step = 256

    @pl.when(jnp.logical_and(pl.program_id(0) == 0, pl.program_id(1) == 0))
    def _():
        pick = lax.broadcasted_iota(jnp.int32, (rows, ages), 0) >> 4
        pick = (pick == lax.broadcasted_iota(jnp.int32, (rows, ages), 1)).astype(jnp.bfloat16)
        tall = jnp.dot(pick, age_ref[...], preferred_element_type=jnp.float32).astype(jnp.bfloat16)
        spread = lax.broadcasted_iota(jnp.int32, (ages, rows), 1) >> 4
        spread = (spread == lax.broadcasted_iota(jnp.int32, (ages, rows), 0)).astype(jnp.bfloat16)
        for lo in range(0, rows, step):
            hi = min(lo + step, rows)
            both = jnp.dot(tall[lo:hi], spread[:, :hi], preferred_element_type=jnp.float32)
            same = (lax.broadcasted_iota(jnp.int32, both.shape, 0) & 15) == (
                lax.broadcasted_iota(jnp.int32, both.shape, 1) & 15
            )
            wide_ref[lo:hi, :hi] = jnp.where(same, both, 0.0).astype(jnp.bfloat16)

    for lo in range(0, rows, step):
        hi = min(lo + step, rows)
        o_ref[0, lo:hi, :] = jnp.dot(
            wide_ref[lo:hi, :hi], x_ref[0, :hi, :], preferred_element_type=jnp.float32
        ).astype(jnp.bfloat16)


def age_mix(age_factor, noise):
    sexes, rows, cols = noise.shape
    ages = age_factor.shape[0]
    width = 256
    return pl.pallas_call(
        age_mix_kernel,
        out_shape=jax.ShapeDtypeStruct(noise.shape, jnp.bfloat16),
        grid=(sexes, cols // width),
        in_specs=[
            pl.BlockSpec((ages, ages), lambda s, k: (0, 0)),
            pl.BlockSpec((1, rows, width), lambda s, k: (s, 0, k)),
        ],
        out_specs=pl.BlockSpec((1, rows, width), lambda s, k: (s, 0, k)),
        scratch_shapes=[pltpu.VMEM((rows, rows), jnp.bfloat16)],
        compiler_params=pltpu.CompilerParams(vmem_limit_bytes=40 << 20),
        cost_estimate=pl.CostEstimate(
            flops=rows * rows * cols * sexes, bytes_accessed=4 * sexes * rows * cols, transcendentals=0
        ),
        name="age_mix",
    )(age_factor, noise)


def merge_pair(pair, odd_device, swapped):
    axis = pair.ndim - 1
    turned = pltpu.roll(pair, HALF, axis)
    first = jnp.where(odd_device, turned, pair)
    second = jnp.where(odd_device, pair, turned)
    low = lax.broadcasted_iota(jnp.int32, pair.shape[:-2] + (1, LANES), axis) < HALF
    s = 1 if swapped else 0
    return jnp.where(low, first[..., s : s + 1, :], second[..., 1 - s : 2 - s, :])


def loc_mix_kernel(e_ref, x_ref, *refs):
    factors, means, outs = refs[:4], refs[4:8], refs[8:]
    l0, l1, l2, l3 = [f[...] for f in factors]
    r0 = lax.dot_general(
        x_ref[0], jnp.concatenate([l0, l1, l2, l3], 0), NT, preferred_element_type=jnp.float32
    )
    r1 = lax.dot_general(
        x_ref[1], jnp.concatenate([l1, l0, l3, l2], 0), NT, preferred_element_type=jnp.float32
    )
    ages, rows, _ = outs[0].shape
    low = lax.broadcasted_iota(jnp.int32, (1, LANES), 1) < HALF
    for q in range(4):
        g = (q // 2) * LANES
        a, b = r0[:, g : g + LANES], r1[:, g : g + LANES]
        v = jnp.where(low, a, b) if q % 2 == 0 else jnp.where(low, b, a)
        m = merge_pair(means[q][...], (e_ref[q] & 1) == 1, q % 2 == 1)
        outs[q][...] = (v.reshape(ages, rows, LANES) + m).astype(jnp.bfloat16)


def loc_mix(dests, mixed, factors, mean_t):
    sexes, rows, cols = mixed.shape
    ages = mean_t.shape[0]
    steps = 3
    block = ages // steps
    per_age = rows // ages
    msg = jax.ShapeDtypeStruct((ages, per_age, LANES), jnp.bfloat16)

    def mean_spec(q):
        return pl.BlockSpec((block, sexes, LANES), lambda i, e: (i, 0, e[q] // 2))

    return pl.pallas_call(
        loc_mix_kernel,
        out_shape=[msg] * 4,
        grid_spec=pltpu.PrefetchScalarGridSpec(
            num_scalar_prefetch=1,
            grid=(steps,),
            in_specs=[pl.BlockSpec((sexes, block * per_age, cols), lambda i, e: (0, i, 0))]
            + [pl.BlockSpec((HALF, cols), lambda i, e: (0, 0))] * 4
            + [mean_spec(q) for q in range(4)],
            out_specs=[pl.BlockSpec((block, per_age, LANES), lambda i, e: (i, 0, 0))] * 4,
        ),
        compiler_params=pltpu.CompilerParams(vmem_limit_bytes=40 << 20),
        cost_estimate=pl.CostEstimate(
            flops=2 * sexes * rows * cols * 256,
            bytes_accessed=2 * sexes * rows * cols + 8 * rows * LANES,
            transcendentals=0,
        ),
        name="loc_mix",
    )(dests, mixed, *factors, *([mean_t] * 4))


def survive_kernel(first, last, e_ref, *refs):
    xs, pops, regs = refs[:4], refs[4:8], refs[8:12]
    pos = 12
    if not first:
        wsum_in, psum_in = refs[pos : pos + 2]
        pos += 2
    locs = refs[pos : pos + 4]
    pos += 4
    if last:
        region_ref = refs[pos]
        pos += 1
    wsum_ref, psum_ref = refs[pos : pos + 2]
    hi_ref, lo_ref, pop_ref = refs[pos + 2 : pos + 5]
    ages, rows, _ = xs[0].shape
    odd = [(e_ref[q] & 1) == 1 for q in range(4)]
    zero = jnp.zeros((rows, LANES), jnp.float32)

    def age_step(a, carry):
        hazards, totals = carry
        new_h, new_t = [], []
        at = pl.ds(pl.multiple_of(a * rows, rows), rows)
        for q in range(4):
            lanes = slice(q * LANES, (q + 1) * LANES)
            rate = jnp.exp(xs[q][a].astype(jnp.float32))
            h = hazards[q] + rate
            new_h.append(h)
            new_t.append(totals[q] + jnp.exp(-h))
            pop = merge_pair(pops[q][a], odd[q], q % 2 == 1)
            pop_ref[q, pl.ds(a, 1), :] = pop
            hi, lo = split_bf16(rate * pop)
            hi_ref[at, lanes] = hi
            lo_ref[at, lanes] = lo
        return tuple(new_h), tuple(new_t)

    hazards, totals = lax.fori_loop(0, ages, age_step, ((zero,) * 4, (zero,) * 4))
    for q in range(4):
        out = (totals[q] + (0.5 - 0.5 * jnp.exp(-hazards[q]))) * (1.0 / ages)
        if q % 2 == 1:
            out = pltpu.roll(out, HALF, 1)
        locs[q][...] = out

    lane = lax.broadcasted_iota(jnp.int32, (1, LANES), 1)
    low = lane < HALF
    onehots = []
    for q in range(4):
        pair = regs[q][...]
        turned = pltpu.roll(pair, HALF, 1)
        mine = jnp.where(low, jnp.where(odd[q], turned, pair), jnp.where(odd[q], pair, turned))
        upper = low if q % 2 == 1 else jnp.logical_not(low)
        target = mine + jnp.where(upper, REGIONS, 0)
        region = lax.broadcasted_iota(jnp.int32, (LANES, LANES), 0)
        onehots.append(jnp.where(region == target, 1.0, 0.0).astype(jnp.bfloat16))
    onehot = jnp.concatenate(onehots, 1)

    def regions(x):
        return lax.dot_general(x, onehot, NT, preferred_element_type=jnp.float32)

    pop_hi, pop_lo = split_bf16(jnp.concatenate([pop_ref[q] for q in range(4)], 1))
    wsum = regions(hi_ref[...]) + regions(lo_ref[...])
    psum = regions(pop_hi) + regions(pop_lo)
    if not first:
        wsum = wsum + wsum_in[...]
        psum = psum + psum_in[...]
    wsum_ref[...] = wsum
    psum_ref[...] = psum
    if last:

        def region_step(a, carry):
            h, t = carry
            at = pl.ds(pl.multiple_of(a * rows, rows), rows)
            h = h + wsum_ref[at, :] / psum_ref[pl.ds(a, 1), :]
            return h, t + jnp.exp(-h)

        h, t = lax.fori_loop(0, ages, region_step, (zero, zero))
        region_ref[...] = (t + (0.5 - 0.5 * jnp.exp(-h))) * (1.0 / ages)


def survive(dests, messages, pop_t, region_row, sums, last):
    ages, rows, _ = messages[0].shape
    sexes = pop_t.shape[1]
    first = sums is None
    f32 = jnp.float32
    loc = jax.ShapeDtypeStruct((rows, LANES), f32)
    wsum = jax.ShapeDtypeStruct((ages * rows, LANES), f32)
    psum = jax.ShapeDtypeStruct((ages, LANES), f32)
    whole = lambda *shape: pl.BlockSpec(shape, lambda i, e: (0,) * len(shape))

    def pop_spec(q):
        return pl.BlockSpec((ages, sexes, LANES), lambda i, e: (0, 0, e[q] // 2))

    def region_spec(q):
        return pl.BlockSpec((1, LANES), lambda i, e: (0, e[q] // 2))

    in_specs = [whole(ages, rows, LANES)] * 4
    in_specs += [pop_spec(q) for q in range(4)] + [region_spec(q) for q in range(4)]
    args = list(messages) + [pop_t] * 4 + [region_row] * 4
    sum_specs = [whole(ages * rows, LANES), whole(ages, LANES)]
    outs, out_specs = [loc] * 4, [whole(rows, LANES)] * 4
    if not first:
        in_specs += sum_specs
        args += list(sums)
    if last:
        outs.append(loc)
        out_specs.append(whole(rows, LANES))
    scratch = [
        pltpu.VMEM((ages * rows, 4 * LANES), jnp.bfloat16),
        pltpu.VMEM((ages * rows, 4 * LANES), jnp.bfloat16),
        pltpu.VMEM((4, ages, LANES), f32),
    ]
    if last:
        scratch = [pltpu.VMEM(wsum.shape, f32), pltpu.VMEM(psum.shape, f32)] + scratch
    else:
        outs += [wsum, psum]
        out_specs += sum_specs
    return pl.pallas_call(
        functools.partial(survive_kernel, first, last),
        out_shape=outs,
        grid_spec=pltpu.PrefetchScalarGridSpec(
            num_scalar_prefetch=1,
            grid=(1,),
            in_specs=in_specs,
            out_specs=out_specs,
            scratch_shapes=scratch,
        ),
        compiler_params=pltpu.CompilerParams(vmem_limit_bytes=40 << 20),
        cost_estimate=pl.CostEstimate(
            flops=60 * 4 * ages * rows * LANES,
            bytes_accessed=16 * ages * rows * LANES,
            transcendentals=8 * ages * rows * LANES,
        ),
        name="survive",
    )(dests, *args)


def turn_kernel(near, d_ref, *refs):
    xs, out_ref, order_ref = refs[:8], refs[-2], refs[-1]
    d = d_ref[0]
    ages = xs[0].shape[0]
    for m in range(8):
        order_ref[(d & 7) ^ m] = xs[m][...]
    eye = (
        lax.broadcasted_iota(jnp.int32, (LANES, LANES), 0)
        == lax.broadcasted_iota(jnp.int32, (LANES, LANES), 1)
    ).astype(jnp.bfloat16)
    upper = (lax.broadcasted_iota(jnp.int32, (HALF, LANES), 1) >= HALF).astype(jnp.int32)
    swapped = (upper ^ ((d >> 2) & 1) ^ (1 if near else 0)) == 1
    for a in range(ages):
        tile = order_ref[:, a].reshape(LANES, LANES)
        t = lax.dot_general(eye, tile, NT, preferred_element_type=jnp.float32)
        top, bottom = t[:HALF], t[HALF:]
        out_ref[0, a] = jnp.where(swapped, bottom, top).astype(jnp.bfloat16)
        out_ref[1, a] = jnp.where(swapped, top, bottom).astype(jnp.bfloat16)


def turn(device, messages, out_shape, previous):
    near = previous is None
    ages, rows, _ = messages[0].shape
    steps = 3
    block = ages // steps
    in_specs = [pl.BlockSpec((block, rows, LANES), lambda i, d: (i, 0, 0))] * 8
    args = list(messages)
    flip = 0 if near else 1
    aliases = {}
    if not near:
        in_specs.append(pl.BlockSpec(memory_space=pl.ANY))
        args.append(previous)
        aliases = {9: 0}
    return pl.pallas_call(
        functools.partial(turn_kernel, near),
        out_shape=out_shape,
        grid_spec=pltpu.PrefetchScalarGridSpec(
            num_scalar_prefetch=1,
            grid=(steps,),
            in_specs=in_specs,
            out_specs=pl.BlockSpec((2, block, HALF, LANES), lambda i, d: (0, i, 0, (d[0] // 8) ^ flip)),
            scratch_shapes=[pltpu.VMEM((8, block, rows, LANES), jnp.bfloat16)],
        ),
        input_output_aliases=aliases,
        compiler_params=pltpu.CompilerParams(vmem_limit_bytes=40 << 20),
        cost_estimate=pl.CostEstimate(
            flops=2 * ages * LANES**3, bytes_accessed=32 * ages * rows * LANES, transcendentals=0
        ),
        name="turn",
    )(device, *args)


def shards_sixteen(noise, loc_factor, age_factor, mean_rate, population, region_of):
    sexes, ages, rows, locs = noise.shape
    devices = lax.axis_size("loc")
    here = lax.axis_index("loc")

    def swap(x, bits):
        return lax.ppermute(x, "loc", [(i, i ^ bits) for i in range(devices)])

    mean_t = jnp.transpose(mean_rate, (1, 0, 2))
    pop_t = jnp.transpose(population, (1, 0, 2))
    region_row = region_of.reshape(1, locs)
    dests = [here ^ jnp.array(c, jnp.int32) for c in CHUNKS]

    factors = {0: loc_factor}
    for bits in (8, 12, 4):
        factors[bits] = swap(loc_factor, bits)
    mixed = age_mix(age_factor, noise.reshape(sexes, ages * rows, locs))

    lane0 = jnp.concatenate([factors[b] for b in CHUNKS[0]], 0)
    lane2 = swap(lane0, 2)
    lane1 = swap(lane0, 1)
    lane3 = swap(lane2, 1)
    local = loc_factor.shape[0]
    lanes = [[factors[b] for b in CHUNKS[0]]]
    for whole in (lane2, lane1, lane3):
        lanes.append([whole[i * local : (i + 1) * local] for i in range(4)])

    sent, got = {}, {}
    for c, bits in enumerate(CHUNKS):
        messages = loc_mix(dests[c], mixed, lanes[c], mean_t)
        for b, m in zip(bits, messages):
            sent[b] = m
            got[b] = m if b == 0 else swap(m, b)

    loc_parts, sums = {}, None
    for c, bits in enumerate(CHUNKS):
        last = c == len(CHUNKS) - 1
        out = survive(dests[c], [sent[b] for b in bits], pop_t, region_row, sums, last)
        for b, o in zip(bits, out[:4]):
            loc_parts[b] = o
        if last:
            region_part = out[4]
        else:
            sums = out[4:]

    by_bits = jnp.stack([loc_parts[b] for b in range(devices)])
    by_device = jnp.take(by_bits, here ^ jnp.arange(devices, dtype=jnp.int32), axis=0)
    mine = REGIONS // devices
    region_out = region_part.reshape(rows, sexes, devices, mine)
    region_out = jnp.transpose(region_out, (2, 1, 3, 0)).reshape(devices, 1, sexes * mine * rows)
    small = lax.all_to_all(
        jnp.concatenate([by_device, region_out], axis=1), "loc", split_axis=0, concat_axis=0, tiled=True
    )
    loc_survival = jnp.transpose(small[:, :rows].reshape(devices * rows, LANES), (1, 0)).reshape(
        sexes, local, devices * rows
    )
    region_survival = jnp.transpose(
        small[:, rows].reshape(devices, sexes, mine, rows), (1, 2, 0, 3)
    ).reshape(sexes, mine, devices * rows)

    shape = jax.ShapeDtypeStruct((sexes, ages, local, devices * rows), jnp.bfloat16)
    device = here[None]
    half = turn(device, [got[b] for b in range(8)], shape, None)
    log_rates = turn(device, [got[b] for b in range(8, 16)], shape, half)
    return (log_rates, loc_survival, region_survival)


def shards(noise, loc_factor, *rest):
    sixteen = lax.axis_size("loc") == 16 and noise.shape[2] == 16 and noise.shape[1] % 3 == 0
    if sixteen and noise.shape[0] == 2 and loc_factor.shape == (HALF, 1024):
        return shards_sixteen(noise, loc_factor, *rest)
    return shards_any(noise, loc_factor, *rest)


def solution(mesh):
    placed = (
        P(None, None, ("yr", "loc"), None),
        P("loc", None),
        P(),
        P("yr", None, None),
        P("yr", None, None),
        P(),
    )
    return jax.shard_map(
        shards,
        mesh=mesh,
        in_specs=placed,
        out_specs=(P(None, None, "loc", "yr"), P(None, "loc", "yr"), P(None, "loc", "yr")),
        check_vma=False,
    )
```

```python
import functools

import jax
import jax.numpy as jnp
from jax import lax
from jax.experimental import pallas as pl
from jax.experimental.pallas import tpu as pltpu
from jax.sharding import PartitionSpec as P

REGIONS = 64
LANES = 128
HALF = 64
NT = (((1,), (1,)), ((), ()))
CHUNKS = ((8, 12, 4, 0), (9, 13, 5, 1), (10, 14, 6, 2), (11, 15, 7, 3))
FAR = (8, 12, 9, 13, 10, 14, 11, 15)
NEAR = (4, 5, 1, 6, 2, 7, 3)


def survival(rates):
    hazard = jnp.cumsum(rates, axis=1)
    after = jnp.exp(-hazard)
    total = 0.5 + jnp.sum(after, axis=1) - 0.5 * after[:, -1]
    return total / rates.shape[1]


def shards_any(noise, loc_factor, age_factor, mean_rate, population, region_of):
    highest = lax.Precision.HIGHEST
    spread = jnp.einsum(
        "sark,lk->sarl",
        noise,
        lax.all_gather(loc_factor, "loc", axis=0, tiled=True),
        preferred_element_type=jnp.float32,
    ).astype(jnp.bfloat16)
    mixed = jnp.einsum("ab,sbrl->sarl", age_factor, spread, preferred_element_type=jnp.float32)
    log_section = (mean_rate[:, :, None, :] + mixed).astype(jnp.bfloat16)
    rates = jnp.exp(log_section.astype(jnp.float32))
    onehot = (region_of == jnp.arange(REGIONS, dtype=jnp.int32)[None, :]).astype(jnp.float32)
    totals = jnp.einsum("sal,lg->sag", population, onehot, precision=highest)
    weighted = jnp.einsum(
        "sarl,lg->sarg", population[:, :, None, :] * rates, onehot, precision=highest
    )
    region_section = survival(weighted / totals[:, :, None, :])
    region_moved = lax.all_to_all(region_section, "loc", split_axis=2, concat_axis=1, tiled=True)
    region_survival = jnp.transpose(region_moved, (0, 2, 1))
    turned = jnp.transpose(
        lax.all_to_all(log_section, "loc", split_axis=3, concat_axis=2, tiled=True), (0, 1, 3, 2)
    )
    loc_survival = survival(jnp.exp(turned.astype(jnp.float32)))
    return (turned, loc_survival, region_survival)


def after(x, *others):
    return lax.optimization_barrier((x,) + others)[0]


def split_bf16(x):
    hi = x.astype(jnp.bfloat16)
    return hi, (x - hi.astype(jnp.float32)).astype(jnp.bfloat16)


def age_mix_kernel(age_ref, x_ref, o_ref, wide_ref):
    ages = age_ref.shape[0]
    rows = x_ref.shape[1]
    step = 256

    @pl.when(jnp.logical_and(pl.program_id(0) == 0, pl.program_id(1) == 0))
    def _():
        pick = lax.broadcasted_iota(jnp.int32, (rows, ages), 0) >> 4
        pick = (pick == lax.broadcasted_iota(jnp.int32, (rows, ages), 1)).astype(jnp.bfloat16)
        tall = jnp.dot(pick, age_ref[...], preferred_element_type=jnp.float32).astype(jnp.bfloat16)
        spread = lax.broadcasted_iota(jnp.int32, (ages, rows), 1) >> 4
        spread = (spread == lax.broadcasted_iota(jnp.int32, (ages, rows), 0)).astype(jnp.bfloat16)
        for lo in range(0, rows, step):
            hi = min(lo + step, rows)
            both = jnp.dot(tall[lo:hi], spread[:, :hi], preferred_element_type=jnp.float32)
            same = (lax.broadcasted_iota(jnp.int32, both.shape, 0) & 15) == (
                lax.broadcasted_iota(jnp.int32, both.shape, 1) & 15
            )
            wide_ref[lo:hi, :hi] = jnp.where(same, both, 0.0).astype(jnp.bfloat16)

    for lo in range(0, rows, step):
        hi = min(lo + step, rows)
        o_ref[0, lo:hi, :] = jnp.dot(
            wide_ref[lo:hi, :hi], x_ref[0, :hi, :], preferred_element_type=jnp.float32
        ).astype(jnp.bfloat16)


def age_mix(age_factor, noise):
    sexes, rows, cols = noise.shape
    ages = age_factor.shape[0]
    width = 512
    return pl.pallas_call(
        age_mix_kernel,
        out_shape=jax.ShapeDtypeStruct(noise.shape, jnp.bfloat16),
        grid=(sexes, cols // width),
        in_specs=[
            pl.BlockSpec((ages, ages), lambda s, k: (0, 0)),
            pl.BlockSpec((1, rows, width), lambda s, k: (s, 0, k)),
        ],
        out_specs=pl.BlockSpec((1, rows, width), lambda s, k: (s, 0, k)),
        scratch_shapes=[pltpu.VMEM((rows, rows), jnp.bfloat16)],
        compiler_params=pltpu.CompilerParams(vmem_limit_bytes=60 << 20),
        cost_estimate=pl.CostEstimate(
            flops=rows * rows * cols * sexes, bytes_accessed=4 * sexes * rows * cols, transcendentals=0
        ),
        name="age_mix",
    )(age_factor, noise)


def merge_pair(pair, odd_device, swapped):
    axis = pair.ndim - 1
    turned = pltpu.roll(pair, HALF, axis)
    first = jnp.where(odd_device, turned, pair)
    second = jnp.where(odd_device, pair, turned)
    low = lax.broadcasted_iota(jnp.int32, pair.shape[:-2] + (1, LANES), axis) < HALF
    s = 1 if swapped else 0
    return jnp.where(low, first[..., s : s + 1, :], second[..., 1 - s : 2 - s, :])


def loc_mix_kernel(bits, d_ref, x_ref, *refs):
    factors, means, outs = refs[:4], refs[4:8], refs[8:]
    l0, l1, l2, l3 = [f[...] for f in factors]
    r0 = lax.dot_general(
        x_ref[0], jnp.concatenate([l0, l1, l2, l3], 0), NT, preferred_element_type=jnp.float32
    )
    r1 = lax.dot_general(
        x_ref[1], jnp.concatenate([l1, l0, l3, l2], 0), NT, preferred_element_type=jnp.float32
    )
    ages, rows, _ = outs[0].shape
    low = lax.broadcasted_iota(jnp.int32, (1, LANES), 1) < HALF
    for q in range(4):
        g = (q // 2) * LANES
        a, b = r0[:, g : g + LANES], r1[:, g : g + LANES]
        v = jnp.where(low, a, b) if q % 2 == 0 else jnp.where(low, b, a)
        m = merge_pair(means[q][...], ((d_ref[0] ^ bits[q]) & 1) == 1, q % 2 == 1)
        outs[q][...] = (v.reshape(ages, rows, LANES) + m).astype(jnp.bfloat16)


def loc_mix(device, bits, mixed, factors, mean_t):
    sexes, rows, cols = mixed.shape
    ages = mean_t.shape[0]
    steps = 3
    block = ages // steps
    per_age = rows // ages
    msg = jax.ShapeDtypeStruct((ages, per_age, LANES), jnp.bfloat16)

    def mean_spec(q):
        return pl.BlockSpec((block, sexes, LANES), lambda i, d: (i, 0, (d[0] ^ bits[q]) // 2))

    return pl.pallas_call(
        functools.partial(loc_mix_kernel, bits),
        out_shape=[msg] * 4,
        grid_spec=pltpu.PrefetchScalarGridSpec(
            num_scalar_prefetch=1,
            grid=(steps,),
            in_specs=[pl.BlockSpec((sexes, block * per_age, cols), lambda i, e: (0, i, 0))]
            + [pl.BlockSpec((HALF, cols), lambda i, e: (0, 0))] * 4
            + [mean_spec(q) for q in range(4)],
            out_specs=[pl.BlockSpec((block, per_age, LANES), lambda i, e: (i, 0, 0))] * 4,
        ),
        compiler_params=pltpu.CompilerParams(vmem_limit_bytes=40 << 20),
        cost_estimate=pl.CostEstimate(
            flops=2 * sexes * rows * cols * 256,
            bytes_accessed=2 * sexes * rows * cols + 8 * rows * LANES,
            transcendentals=0,
        ),
        name="loc_mix",
    )(device, mixed, *factors, *([mean_t] * 4))


def survive_kernel(bits, first, last, d_ref, *refs):
    xs, pops, regs = refs[:4], refs[4:8], refs[8:12]
    pos = 12
    if not first:
        locs_in, wsum_in, psum_in = refs[pos : pos + 3]
        pos += 3
    locs = refs[pos]
    pos += 1
    if not first:
        locs[...] = locs_in[...]
    if last:
        region_ref = refs[pos]
        pos += 1
    wsum_ref, psum_ref = refs[pos : pos + 2]
    hi_ref, lo_ref, pop_ref = refs[pos + 2 : pos + 5]
    ages, rows, _ = xs[0].shape
    dests = [d_ref[0] ^ b for b in bits]
    odd = [(e & 1) == 1 for e in dests]
    zero = jnp.zeros((rows, LANES), jnp.float32)

    def age_step(a, carry):
        hazards, totals = carry
        new_h, new_t = [], []
        at = pl.ds(pl.multiple_of(a * rows, rows), rows)
        for q in range(4):
            lanes = slice(q * LANES, (q + 1) * LANES)
            rate = jnp.exp(xs[q][a].astype(jnp.float32))
            h = hazards[q] + rate
            new_h.append(h)
            new_t.append(totals[q] + jnp.exp(-h))
            pop = merge_pair(pops[q][a], odd[q], q % 2 == 1)
            pop_ref[q, pl.ds(a, 1), :] = pop
            hi, lo = split_bf16(rate * pop)
            hi_ref[at, lanes] = hi
            lo_ref[at, lanes] = lo
        return tuple(new_h), tuple(new_t)

    hazards, totals = lax.fori_loop(0, ages, age_step, ((zero,) * 4, (zero,) * 4), unroll=3)
    for q in range(4):
        out = (totals[q] + (0.5 - 0.5 * jnp.exp(-hazards[q]))) * (1.0 / ages)
        if q % 2 == 1:
            out = pltpu.roll(out, HALF, 1)
        locs[dests[q]] = out

    lane = lax.broadcasted_iota(jnp.int32, (1, LANES), 1)
    low = lane < HALF
    onehots = []
    for q in range(4):
        pair = regs[q][...]
        turned = pltpu.roll(pair, HALF, 1)
        mine = jnp.where(low, jnp.where(odd[q], turned, pair), jnp.where(odd[q], pair, turned))
        upper = low if q % 2 == 1 else jnp.logical_not(low)
        target = mine + jnp.where(upper, REGIONS, 0)
        region = lax.broadcasted_iota(jnp.int32, (LANES, LANES), 0)
        onehots.append(jnp.where(region == target, 1.0, 0.0).astype(jnp.bfloat16))
    onehot = jnp.concatenate(onehots, 1)

    def regions(x):
        return lax.dot_general(x, onehot, NT, preferred_element_type=jnp.float32)

    pop_hi, pop_lo = split_bf16(jnp.concatenate([pop_ref[q] for q in range(4)], 1))
    wsum = regions(hi_ref[...]) + regions(lo_ref[...])
    psum = regions(pop_hi) + regions(pop_lo)
    if not first:
        wsum = wsum + wsum_in[...]
        psum = psum + psum_in[...]
    wsum_ref[...] = wsum
    psum_ref[...] = psum
    if last:

        def region_step(a, carry):
            h, t = carry
            at = pl.ds(pl.multiple_of(a * rows, rows), rows)
            h = h + wsum_ref[at, :] / psum_ref[pl.ds(a, 1), :]
            return h, t + jnp.exp(-h)

        h, t = lax.fori_loop(0, ages, region_step, (zero, zero), unroll=3)
        region_ref[...] = (t + (0.5 - 0.5 * jnp.exp(-h))) * (1.0 / ages)


def survive(device, bits, messages, pop_t, region_row, sums, last):
    ages, rows, _ = messages[0].shape
    sexes, locs = pop_t.shape[1], pop_t.shape[2] // HALF
    first = sums is None
    f32 = jnp.float32
    loc = jax.ShapeDtypeStruct((locs, rows, LANES), f32)
    wsum = jax.ShapeDtypeStruct((ages * rows, LANES), f32)
    psum = jax.ShapeDtypeStruct((ages, LANES), f32)
    whole = lambda *shape: pl.BlockSpec(shape, lambda i, e: (0,) * len(shape))

    def pop_spec(q):
        return pl.BlockSpec((ages, sexes, LANES), lambda i, d: (0, 0, (d[0] ^ bits[q]) // 2))

    def region_spec(q):
        return pl.BlockSpec((1, LANES), lambda i, d: (0, (d[0] ^ bits[q]) // 2))

    in_specs = [whole(ages, rows, LANES)] * 4
    in_specs += [pop_spec(q) for q in range(4)] + [region_spec(q) for q in range(4)]
    args = list(messages) + [pop_t] * 4 + [region_row] * 4
    sum_specs = [whole(ages * rows, LANES), whole(ages, LANES)]
    outs, out_specs = [loc], [whole(locs, rows, LANES)]
    if not first:
        in_specs += out_specs + sum_specs
        args += list(sums)
    if last:
        outs.append(jax.ShapeDtypeStruct((rows, LANES), f32))
        out_specs.append(whole(rows, LANES))
    scratch = [
        pltpu.VMEM((ages * rows, 4 * LANES), jnp.bfloat16),
        pltpu.VMEM((ages * rows, 4 * LANES), jnp.bfloat16),
        pltpu.VMEM((4, ages, LANES), f32),
    ]
    if last:
        scratch = [pltpu.VMEM(wsum.shape, f32), pltpu.VMEM(psum.shape, f32)] + scratch
    else:
        outs += [wsum, psum]
        out_specs += sum_specs
    return pl.pallas_call(
        functools.partial(survive_kernel, bits, first, last),
        out_shape=outs,
        grid_spec=pltpu.PrefetchScalarGridSpec(
            num_scalar_prefetch=1,
            grid=(1,),
            in_specs=in_specs,
            out_specs=out_specs,
            scratch_shapes=scratch,
        ),
        compiler_params=pltpu.CompilerParams(vmem_limit_bytes=40 << 20),
        cost_estimate=pl.CostEstimate(
            flops=60 * 4 * ages * rows * LANES,
            bytes_accessed=16 * ages * rows * LANES,
            transcendentals=8 * ages * rows * LANES,
        ),
        name="survive",
    )(device, *args)


def turn_kernel(near, d_ref, *refs):
    xs, out_ref, order_ref = refs[:8], refs[-2], refs[-1]
    d = d_ref[0]
    ages = xs[0].shape[0]
    for m in range(8):
        order_ref[(d & 7) ^ m] = xs[m][...]
    upper = (lax.broadcasted_iota(jnp.int32, (HALF, LANES), 1) >= HALF).astype(jnp.int32)
    swapped = (upper ^ ((d >> 2) & 1) ^ (1 if near else 0)) == 1
    for a in range(ages):
        tile = order_ref[:, a].reshape(LANES, LANES)
        t = tile.T.astype(jnp.float32)
        top, bottom = t[:HALF], t[HALF:]
        out_ref[0, a] = jnp.where(swapped, bottom, top).astype(jnp.bfloat16)
        out_ref[1, a] = jnp.where(swapped, top, bottom).astype(jnp.bfloat16)


def turn(device, messages, out_shape, previous):
    near = previous is None
    ages, rows, _ = messages[0].shape
    steps = 3
    block = ages // steps
    in_specs = [pl.BlockSpec((block, rows, LANES), lambda i, d: (i, 0, 0))] * 8
    args = list(messages)
    flip = 0 if near else 1
    aliases = {}
    if not near:
        in_specs.append(pl.BlockSpec(memory_space=pl.ANY))
        args.append(previous)
        aliases = {9: 0}
    return pl.pallas_call(
        functools.partial(turn_kernel, near),
        out_shape=out_shape,
        grid_spec=pltpu.PrefetchScalarGridSpec(
            num_scalar_prefetch=1,
            grid=(steps,),
            in_specs=in_specs,
            out_specs=pl.BlockSpec((2, block, HALF, LANES), lambda i, d: (0, i, 0, (d[0] // 8) ^ flip)),
            scratch_shapes=[pltpu.VMEM((8, block, rows, LANES), jnp.bfloat16)],
        ),
        input_output_aliases=aliases,
        compiler_params=pltpu.CompilerParams(vmem_limit_bytes=40 << 20),
        cost_estimate=pl.CostEstimate(
            flops=2 * ages * LANES**3, bytes_accessed=32 * ages * rows * LANES, transcendentals=0
        ),
        name="turn",
    )(device, *args)


def shards_sixteen(noise, loc_factor, age_factor, mean_rate, population, region_of):
    sexes, ages, rows, locs = noise.shape
    devices = lax.axis_size("loc")
    here = lax.axis_index("loc")

    def swap(x, bits):
        return lax.ppermute(x, "loc", [(i, i ^ bits) for i in range(devices)])

    mean_t = jnp.transpose(mean_rate, (1, 0, 2))
    pop_t = jnp.transpose(population, (1, 0, 2))
    region_row = region_of.reshape(1, locs)
    device = here[None]
    local = loc_factor.shape[0]

    factors = {0: loc_factor}
    for bits in (8, 12, 4):
        factors[bits] = swap(loc_factor, bits)
    mixed = age_mix(age_factor, noise.reshape(sexes, ages * rows, locs))

    def pieces(whole):
        return [whole[i * local : (i + 1) * local] for i in range(4)]

    lane0 = [factors[b] for b in CHUNKS[0]]
    joined = jnp.concatenate(lane0, 0)
    lane1 = swap(joined, 1)
    lane2 = swap(joined, 2)
    lane3 = swap(lane2, 1)
    sent = {}
    for bits, lane in zip(CHUNKS, (lane0, pieces(lane1), pieces(lane2), pieces(lane3))):
        sent.update(zip(bits, loc_mix(device, bits, mixed, lane, mean_t)))

    got = {0: sent[0]}
    for order, window in ((FAR, 3), (NEAR, 2)):
        for i, b in enumerate(order):
            message = sent[b] if i < window else after(sent[b], got[order[i - window]])
            got[b] = swap(message, b)

    sums = None
    for c, bits in enumerate(CHUNKS):
        messages = [sent[b] for b in bits]
        if c == 0:
            messages[0] = after(messages[0], sent[CHUNKS[3][3]])
        else:
            messages[0] = after(messages[0], got[FAR[c - 1]])
        sums = survive(device, bits, messages, pop_t, region_row, sums, c == len(CHUNKS) - 1)
    by_device, region_part = sums

    mine = REGIONS // devices
    region_out = region_part.reshape(rows, sexes, devices, mine)
    region_out = jnp.transpose(region_out, (2, 1, 3, 0)).reshape(devices, 1, sexes * mine * rows)
    packed = jnp.concatenate([by_device, region_out], axis=1)
    small = lax.all_to_all(packed, "loc", split_axis=0, concat_axis=0, tiled=True)
    loc_survival = jnp.transpose(small[:, :rows].reshape(devices * rows, LANES), (1, 0)).reshape(
        sexes, local, devices * rows
    )
    region_survival = jnp.transpose(
        small[:, rows].reshape(devices, sexes, mine, rows), (1, 2, 0, 3)
    ).reshape(sexes, mine, devices * rows)

    shape = jax.ShapeDtypeStruct((sexes, ages, local, devices * rows), jnp.bfloat16)
    close = [got[b] for b in range(8)]
    close[0] = after(close[0], packed)
    half = turn(device, close, shape, None)
    log_rates = turn(device, [got[b] for b in range(8, 16)], shape, half)
    return (log_rates, loc_survival, region_survival)


def shards(noise, loc_factor, *rest):
    sixteen = lax.axis_size("loc") == 16 and noise.shape[2] == 16 and noise.shape[1] % 3 == 0
    if sixteen and noise.shape[0] == 2 and loc_factor.shape == (HALF, 1024):
        return shards_sixteen(noise, loc_factor, *rest)
    return shards_any(noise, loc_factor, *rest)


def solution(mesh):
    placed = (
        P(None, None, ("yr", "loc"), None),
        P("loc", None),
        P(),
        P("yr", None, None),
        P("yr", None, None),
        P(),
    )
    return jax.shard_map(
        shards,
        mesh=mesh,
        in_specs=placed,
        out_specs=(P(None, None, "loc", "yr"), P(None, "loc", "yr"), P(None, "loc", "yr")),
        check_vma=False,
    )
```

```python
import functools

import jax
import jax.numpy as jnp
from jax import lax
from jax.experimental import pallas as pl
from jax.experimental.pallas import tpu as pltpu
from jax.sharding import PartitionSpec as P

REGIONS = 64
LANES = 128
HALF = 64
NT = (((1,), (1,)), ((), ()))
CHUNKS = ((8, 12, 4, 0), (9, 13, 5, 1), (10, 14, 6, 2), (11, 15, 7, 3))
FAR = (8, 12, 9, 13, 10, 14, 11, 15)
NEAR = (4, 5, 1, 6, 2, 7, 3)


def survival(rates):
    hazard = jnp.cumsum(rates, axis=1)
    after = jnp.exp(-hazard)
    total = 0.5 + jnp.sum(after, axis=1) - 0.5 * after[:, -1]
    return total / rates.shape[1]


def shards_any(noise, loc_factor, age_factor, mean_rate, population, region_of):
    highest = lax.Precision.HIGHEST
    spread = jnp.einsum(
        "sark,lk->sarl",
        noise,
        lax.all_gather(loc_factor, "loc", axis=0, tiled=True),
        preferred_element_type=jnp.float32,
    ).astype(jnp.bfloat16)
    mixed = jnp.einsum("ab,sbrl->sarl", age_factor, spread, preferred_element_type=jnp.float32)
    log_section = (mean_rate[:, :, None, :] + mixed).astype(jnp.bfloat16)
    rates = jnp.exp(log_section.astype(jnp.float32))
    onehot = (region_of == jnp.arange(REGIONS, dtype=jnp.int32)[None, :]).astype(jnp.float32)
    totals = jnp.einsum("sal,lg->sag", population, onehot, precision=highest)
    weighted = jnp.einsum(
        "sarl,lg->sarg", population[:, :, None, :] * rates, onehot, precision=highest
    )
    region_section = survival(weighted / totals[:, :, None, :])
    region_moved = lax.all_to_all(region_section, "loc", split_axis=2, concat_axis=1, tiled=True)
    region_survival = jnp.transpose(region_moved, (0, 2, 1))
    turned = jnp.transpose(
        lax.all_to_all(log_section, "loc", split_axis=3, concat_axis=2, tiled=True), (0, 1, 3, 2)
    )
    loc_survival = survival(jnp.exp(turned.astype(jnp.float32)))
    return (turned, loc_survival, region_survival)


def tie(x, other):
    return lax.optimization_barrier((x, other))


def split_bf16(x):
    hi = x.astype(jnp.bfloat16)
    return hi, (x - hi.astype(jnp.float32)).astype(jnp.bfloat16)


def age_mix_kernel(age_ref, x_ref, o_ref, done_ref, wide_ref):
    ages = age_ref.shape[0]
    rows = x_ref.shape[1]
    step = 256

    @pl.when(jnp.logical_and(pl.program_id(0) == 0, pl.program_id(1) == 0))
    def _():
        pick = lax.broadcasted_iota(jnp.int32, (rows, ages), 0) >> 4
        pick = (pick == lax.broadcasted_iota(jnp.int32, (rows, ages), 1)).astype(jnp.bfloat16)
        tall = jnp.dot(pick, age_ref[...], preferred_element_type=jnp.float32).astype(jnp.bfloat16)
        spread = lax.broadcasted_iota(jnp.int32, (ages, rows), 1) >> 4
        spread = (spread == lax.broadcasted_iota(jnp.int32, (ages, rows), 0)).astype(jnp.bfloat16)
        for lo in range(0, rows, step):
            hi = min(lo + step, rows)
            both = jnp.dot(tall[lo:hi], spread[:, :hi], preferred_element_type=jnp.float32)
            same = (lax.broadcasted_iota(jnp.int32, both.shape, 0) & 15) == (
                lax.broadcasted_iota(jnp.int32, both.shape, 1) & 15
            )
            wide_ref[lo:hi, :hi] = jnp.where(same, both, 0.0).astype(jnp.bfloat16)

    done_ref[...] = jnp.zeros_like(done_ref)
    for lo in range(0, rows, step):
        hi = min(lo + step, rows)
        o_ref[0, lo:hi, :] = jnp.dot(
            wide_ref[lo:hi, :hi], x_ref[0, :hi, :], preferred_element_type=jnp.float32
        ).astype(jnp.bfloat16)


def age_mix(age_factor, noise):
    sexes, rows, cols = noise.shape
    ages = age_factor.shape[0]
    width = 512
    return pl.pallas_call(
        age_mix_kernel,
        out_shape=(jax.ShapeDtypeStruct(noise.shape, jnp.bfloat16), jax.ShapeDtypeStruct((8, LANES), jnp.float32)),
        grid=(sexes, cols // width),
        in_specs=[
            pl.BlockSpec((ages, ages), lambda s, k: (0, 0)),
            pl.BlockSpec((1, rows, width), lambda s, k: (s, 0, k)),
        ],
        out_specs=(pl.BlockSpec((1, rows, width), lambda s, k: (s, 0, k)), pl.BlockSpec((8, LANES), lambda s, k: (0, 0))),
        scratch_shapes=[pltpu.VMEM((rows, rows), jnp.bfloat16)],
        compiler_params=pltpu.CompilerParams(vmem_limit_bytes=60 << 20),
        cost_estimate=pl.CostEstimate(
            flops=rows * rows * cols * sexes, bytes_accessed=4 * sexes * rows * cols, transcendentals=0
        ),
        name="age_mix",
    )(age_factor, noise)


def merge_pair(pair, odd_device, swapped):
    axis = pair.ndim - 1
    turned = pltpu.roll(pair, HALF, axis)
    first = jnp.where(odd_device, turned, pair)
    second = jnp.where(odd_device, pair, turned)
    low = lax.broadcasted_iota(jnp.int32, pair.shape[:-2] + (1, LANES), axis) < HALF
    s = 1 if swapped else 0
    return jnp.where(low, first[..., s : s + 1, :], second[..., 1 - s : 2 - s, :])


def join_kernel(*refs):
    size = refs[0].shape[0]
    for i, ref in enumerate(refs[:-1]):
        refs[-1][i * size : (i + 1) * size, :] = ref[...]


def join(parts):
    rows, cols = parts[0].shape
    return pl.pallas_call(
        join_kernel,
        out_shape=jax.ShapeDtypeStruct((rows * len(parts), cols), parts[0].dtype),
        compiler_params=pltpu.CompilerParams(vmem_limit_bytes=60 << 20),
        cost_estimate=pl.CostEstimate(
            flops=0, bytes_accessed=4 * len(parts) * rows * cols, transcendentals=0
        ),
        name="join",
    )(*parts)


def loc_mix_kernel(bits, d_ref, x_ref, l_ref, m0, m1, m2, m3, done_ref, *outs):
    factor = l_ref[...]
    crossed = jnp.concatenate(
        [l_ref[at * HALF : (at + 1) * HALF, :] for at in (1, 0, 3, 2)], 0
    )
    means = (m0, m1, m2, m3)
    ages, rows, _ = outs[0].shape
    r0 = lax.dot_general(x_ref[0], factor, NT, preferred_element_type=jnp.float32)
    r1 = lax.dot_general(x_ref[1], crossed, NT, preferred_element_type=jnp.float32)
    low = lax.broadcasted_iota(jnp.int32, (1, LANES), 1) < HALF
    for q in range(4):
        g = (q // 2) * LANES
        a, b = r0[:, g : g + LANES], r1[:, g : g + LANES]
        v = jnp.where(low, a, b) if q % 2 == 0 else jnp.where(low, b, a)
        m = merge_pair(means[q][...], ((d_ref[0] ^ bits[q]) & 1) == 1, q % 2 == 1)
        outs[q][...] = (v.reshape(ages, rows, LANES) + m).astype(jnp.bfloat16)


def loc_mix(device, bits, mixed, factor, mean_t, done):
    sexes, rows, cols = mixed.shape
    ages = mean_t.shape[0]
    steps = 3
    block = ages // steps
    per_age = rows // ages
    msg = jax.ShapeDtypeStruct((ages, per_age, LANES), jnp.bfloat16)

    def mean_spec(q):
        return pl.BlockSpec((block, sexes, LANES), lambda i, d: (i, 0, (d[0] ^ bits[q]) // 2))

    return pl.pallas_call(
        functools.partial(loc_mix_kernel, bits),
        out_shape=[msg] * 4,
        grid_spec=pltpu.PrefetchScalarGridSpec(
            num_scalar_prefetch=1,
            grid=(steps,),
            in_specs=[pl.BlockSpec((sexes, block * per_age, cols), lambda i, d: (0, i, 0))]
            + [pl.BlockSpec(factor.shape, lambda i, d: (0, 0))]
            + [mean_spec(q) for q in range(4)]
            + [pl.BlockSpec(done.shape, lambda i, d: (0, 0))],
            out_specs=[pl.BlockSpec((block, per_age, LANES), lambda i, d: (i, 0, 0))] * 4,
        ),
        compiler_params=pltpu.CompilerParams(vmem_limit_bytes=60 << 20),
        cost_estimate=pl.CostEstimate(
            flops=2 * sexes * rows * cols * 256,
            bytes_accessed=2 * sexes * rows * cols + 8 * rows * LANES,
            transcendentals=0,
        ),
        name="loc_mix",
    )(device, mixed, factor, *([mean_t] * 4), done)


def survive_kernel(bits, first, last, d_ref, *refs):
    xs, pops, regs = refs[:4], refs[4:8], refs[8:12]
    pos = 12
    if not first:
        locs_in, wsum_in, psum_in = refs[pos : pos + 3]
        pos += 3
    locs = refs[pos]
    pos += 1
    if not first:
        locs[...] = locs_in[...]
    if last:
        region_ref = refs[pos]
        pos += 1
    wsum_ref, psum_ref = refs[pos : pos + 2]
    hi_ref, lo_ref, pop_ref = refs[pos + 2 : pos + 5]
    ages, rows, _ = xs[0].shape
    dests = [d_ref[0] ^ b for b in bits]
    odd = [(e & 1) == 1 for e in dests]
    zero = jnp.zeros((rows, LANES), jnp.float32)

    def age_step(a, carry):
        hazards, totals = carry
        new_h, new_t = [], []
        at = pl.ds(pl.multiple_of(a * rows, rows), rows)
        for q in range(4):
            lanes = slice(q * LANES, (q + 1) * LANES)
            rate = jnp.exp(xs[q][a].astype(jnp.float32))
            h = hazards[q] + rate
            new_h.append(h)
            new_t.append(totals[q] + jnp.exp(-h))
            pop = merge_pair(pops[q][a], odd[q], q % 2 == 1)
            pop_ref[q, pl.ds(a, 1), :] = pop
            hi, lo = split_bf16(rate * pop)
            hi_ref[at, lanes] = hi
            lo_ref[at, lanes] = lo
        return tuple(new_h), tuple(new_t)

    hazards, totals = lax.fori_loop(0, ages, age_step, ((zero,) * 4, (zero,) * 4), unroll=3)
    for q in range(4):
        out = (totals[q] + (0.5 - 0.5 * jnp.exp(-hazards[q]))) * (1.0 / ages)
        if q % 2 == 1:
            out = pltpu.roll(out, HALF, 1)
        locs[dests[q]] = out

    lane = lax.broadcasted_iota(jnp.int32, (1, LANES), 1)
    low = lane < HALF
    onehots = []
    for q in range(4):
        pair = regs[q][...]
        turned = pltpu.roll(pair, HALF, 1)
        mine = jnp.where(low, jnp.where(odd[q], turned, pair), jnp.where(odd[q], pair, turned))
        upper = low if q % 2 == 1 else jnp.logical_not(low)
        target = mine + jnp.where(upper, REGIONS, 0)
        region = lax.broadcasted_iota(jnp.int32, (LANES, LANES), 0)
        onehots.append(jnp.where(region == target, 1.0, 0.0).astype(jnp.bfloat16))
    onehot = jnp.concatenate(onehots, 1)

    def regions(x):
        return lax.dot_general(x, onehot, NT, preferred_element_type=jnp.float32)

    pop_hi, pop_lo = split_bf16(jnp.concatenate([pop_ref[q] for q in range(4)], 1))
    wsum = regions(hi_ref[...]) + regions(lo_ref[...])
    psum = regions(pop_hi) + regions(pop_lo)
    if not first:
        wsum = wsum + wsum_in[...]
        psum = psum + psum_in[...]
    wsum_ref[...] = wsum
    psum_ref[...] = psum
    if last:

        def region_step(a, carry):
            h, t = carry
            at = pl.ds(pl.multiple_of(a * rows, rows), rows)
            h = h + wsum_ref[at, :] / psum_ref[pl.ds(a, 1), :]
            return h, t + jnp.exp(-h)

        h, t = lax.fori_loop(0, ages, region_step, (zero, zero), unroll=3)
        region_ref[...] = (t + (0.5 - 0.5 * jnp.exp(-h))) * (1.0 / ages)


def survive(device, bits, messages, pop_t, region_row, sums, last):
    ages, rows, _ = messages[0].shape
    sexes, locs = pop_t.shape[1], pop_t.shape[2] // HALF
    first = sums is None
    f32 = jnp.float32
    loc = jax.ShapeDtypeStruct((locs, rows, LANES), f32)
    wsum = jax.ShapeDtypeStruct((ages * rows, LANES), f32)
    psum = jax.ShapeDtypeStruct((ages, LANES), f32)
    whole = lambda *shape: pl.BlockSpec(shape, lambda i, d: (0,) * len(shape))

    def pop_spec(q):
        return pl.BlockSpec((ages, sexes, LANES), lambda i, d: (0, 0, (d[0] ^ bits[q]) // 2))

    def region_spec(q):
        return pl.BlockSpec((1, LANES), lambda i, d: (0, (d[0] ^ bits[q]) // 2))

    in_specs = [whole(ages, rows, LANES)] * 4
    in_specs += [pop_spec(q) for q in range(4)] + [region_spec(q) for q in range(4)]
    args = list(messages) + [pop_t] * 4 + [region_row] * 4
    sum_specs = [whole(ages * rows, LANES), whole(ages, LANES)]
    outs, out_specs = [loc], [whole(locs, rows, LANES)]
    if not first:
        in_specs += out_specs + sum_specs
        args += list(sums)
    if last:
        outs.append(jax.ShapeDtypeStruct((rows, LANES), f32))
        out_specs.append(whole(rows, LANES))
    scratch = [
        pltpu.VMEM((ages * rows, 4 * LANES), jnp.bfloat16),
        pltpu.VMEM((ages * rows, 4 * LANES), jnp.bfloat16),
        pltpu.VMEM((4, ages, LANES), f32),
    ]
    if last:
        scratch = [pltpu.VMEM(wsum.shape, f32), pltpu.VMEM(psum.shape, f32)] + scratch
    else:
        outs += [wsum, psum]
        out_specs += sum_specs
    return pl.pallas_call(
        functools.partial(survive_kernel, bits, first, last),
        out_shape=outs,
        grid_spec=pltpu.PrefetchScalarGridSpec(
            num_scalar_prefetch=1,
            grid=(1,),
            in_specs=in_specs,
            out_specs=out_specs,
            scratch_shapes=scratch,
        ),
        compiler_params=pltpu.CompilerParams(vmem_limit_bytes=60 << 20),
        cost_estimate=pl.CostEstimate(
            flops=60 * 4 * ages * rows * LANES,
            bytes_accessed=16 * ages * rows * LANES,
            transcendentals=8 * ages * rows * LANES,
        ),
        name="survive",
    )(device, *args)


def turn_kernel(near, d_ref, *refs):
    xs, out_ref, order_ref = refs[:8], refs[-2], refs[-1]
    d = d_ref[0]
    ages = xs[0].shape[0]
    for m in range(8):
        order_ref[(d & 7) ^ m] = xs[m][...]
    upper = (lax.broadcasted_iota(jnp.int32, (HALF, LANES), 1) >= HALF).astype(jnp.int32)
    swapped = (upper ^ ((d >> 2) & 1) ^ (1 if near else 0)) == 1
    for a in range(ages):
        tile = order_ref[:, a].reshape(LANES, LANES)
        t = tile.T.astype(jnp.float32)
        top, bottom = t[:HALF], t[HALF:]
        out_ref[0, a] = jnp.where(swapped, bottom, top).astype(jnp.bfloat16)
        out_ref[1, a] = jnp.where(swapped, top, bottom).astype(jnp.bfloat16)


def turn(device, messages, out_shape, previous, ready=()):
    near = previous is None
    ages, rows, _ = messages[0].shape
    steps = 3
    block = ages // steps
    in_specs = [pl.BlockSpec((block, rows, LANES), lambda i, d: (i, 0, 0))] * 8
    args = list(messages)
    flip = 0 if near else 1
    aliases = {}
    if not near:
        in_specs += [pl.BlockSpec(memory_space=pl.ANY)] * (1 + len(ready))
        args += [previous, *ready]
        aliases = {9: 0}
    return pl.pallas_call(
        functools.partial(turn_kernel, near),
        out_shape=out_shape,
        grid_spec=pltpu.PrefetchScalarGridSpec(
            num_scalar_prefetch=1,
            grid=(steps,),
            in_specs=in_specs,
            out_specs=pl.BlockSpec((2, block, HALF, LANES), lambda i, d: (0, i, 0, (d[0] // 8) ^ flip)),
            scratch_shapes=[pltpu.VMEM((8, block, rows, LANES), jnp.bfloat16)],
        ),
        input_output_aliases=aliases,
        compiler_params=pltpu.CompilerParams(vmem_limit_bytes=60 << 20),
        cost_estimate=pl.CostEstimate(
            flops=2 * ages * LANES**3, bytes_accessed=32 * ages * rows * LANES, transcendentals=0
        ),
        name="turn",
    )(device, *args)


def exchange(by_device, region_part, sexes):
    devices, rows, _ = by_device.shape
    mine = REGIONS // devices
    region_out = region_part.reshape(rows, sexes, devices, mine)
    region_out = jnp.transpose(region_out, (2, 1, 3, 0)).reshape(devices, 1, sexes * mine * rows)
    packed = jnp.concatenate([by_device, region_out], axis=1)
    small = lax.all_to_all(packed, "loc", split_axis=0, concat_axis=0, tiled=True)
    loc_survival = jnp.transpose(small[:, :rows].reshape(devices * rows, LANES), (1, 0))
    region_survival = jnp.transpose(
        small[:, rows].reshape(devices, sexes, mine, rows), (1, 2, 0, 3)
    ).reshape(sexes, mine, devices * rows)
    return loc_survival.reshape(sexes, HALF, devices * rows), region_survival


def shards_sixteen(noise, loc_factor, age_factor, mean_rate, population, region_of):
    sexes, ages, rows, locs = noise.shape
    devices = lax.axis_size("loc")
    here = lax.axis_index("loc")

    def swap(x, bits):
        return lax.ppermute(x, "loc", [(i, i ^ bits) for i in range(devices)])

    mean_t = jnp.transpose(mean_rate, (1, 0, 2))
    pop_t = jnp.transpose(population, (1, 0, 2))
    region_row = region_of.reshape(1, locs)
    device = here[None]

    factors = {0: loc_factor}
    for bits in (8, 12, 4):
        factors[bits] = swap(loc_factor, bits)
    mixed, done = age_mix(age_factor, noise.reshape(sexes, ages * rows, locs))
    factors, done = tie(factors, done)

    lane0 = join([factors[b] for b in CHUNKS[0]])
    lane1 = swap(lane0, 1)
    lane2 = swap(lane0, 2)
    lane3 = swap(lane2, 1)
    sent = {}
    for bits, lane in zip(CHUNKS, (lane0, lane1, lane2, lane3)):
        sent.update(zip(bits, loc_mix(device, bits, mixed, lane, mean_t, done)))

    got = {0: sent[0]}
    first, sent[CHUNKS[3][3]] = tie(sent[CHUNKS[0][0]], sent[CHUNKS[3][3]])
    sums = None
    for i, b in enumerate(FAR):
        message = sent[b]
        if i >= 3:
            message, got[FAR[i - 3]] = tie(message, got[FAR[i - 3]])
        if 3 <= i < 7:
            bits = CHUNKS[i - 3]
            messages = [first if b == CHUNKS[0][0] else sent[b] for b in bits]
            sums = survive(device, bits, messages, pop_t, region_row, sums, i == 6)
            message, sums = tie(message, sums)
        if i == 7:
            small = exchange(*sums, sexes)
            message, small = tie(message, small)
        got[b] = swap(message, b)
    for i, b in enumerate(NEAR):
        message = sent[b]
        if i >= 2:
            message, got[NEAR[i - 2]] = tie(message, got[NEAR[i - 2]])
        got[b] = swap(message, b)

    shape = jax.ShapeDtypeStruct((sexes, ages, HALF, devices * rows), jnp.bfloat16)
    close = [got[b] for b in range(8)]
    half = turn(device, close, shape, None)
    loc_survival, region_survival = small
    ready = (loc_survival, region_survival)
    log_rates = turn(device, [got[b] for b in range(8, 16)], shape, half, ready)
    return (log_rates, loc_survival, region_survival)


def shards(noise, loc_factor, *rest):
    sixteen = lax.axis_size("loc") == 16 and noise.shape[2] == 16 and noise.shape[1] % 3 == 0
    if sixteen and noise.shape[0] == 2 and loc_factor.shape == (HALF, 1024):
        return shards_sixteen(noise, loc_factor, *rest)
    return shards_any(noise, loc_factor, *rest)


def solution(mesh):
    placed = (
        P(None, None, ("yr", "loc"), None),
        P("loc", None),
        P(),
        P("yr", None, None),
        P("yr", None, None),
        P(),
    )
    return jax.shard_map(
        shards,
        mesh=mesh,
        in_specs=placed,
        out_specs=(P(None, None, "loc", "yr"), P(None, "loc", "yr"), P(None, "loc", "yr")),
        check_vma=False,
    )
```

```python
import functools

import jax
import jax.numpy as jnp
from jax import lax
from jax.experimental import pallas as pl
from jax.experimental.pallas import tpu as pltpu
from jax.sharding import PartitionSpec as P

REGIONS = 64
LANES = 128
HALF = 64
NT = (((1,), (1,)), ((), ()))
CHUNKS = ((8, 12, 4, 0), (9, 13, 5, 1), (10, 14, 6, 2), (11, 15, 7, 3))
FAR = (8, 12, 9, 13, 10, 14, 11, 15)
NEAR = (4, 5, 1, 6, 2, 7, 3)


def survival(rates):
    hazard = jnp.cumsum(rates, axis=1)
    after = jnp.exp(-hazard)
    total = 0.5 + jnp.sum(after, axis=1) - 0.5 * after[:, -1]
    return total / rates.shape[1]


def shards_any(noise, loc_factor, age_factor, mean_rate, population, region_of):
    highest = lax.Precision.HIGHEST
    spread = jnp.einsum(
        "sark,lk->sarl",
        noise,
        lax.all_gather(loc_factor, "loc", axis=0, tiled=True),
        preferred_element_type=jnp.float32,
    ).astype(jnp.bfloat16)
    mixed = jnp.einsum("ab,sbrl->sarl", age_factor, spread, preferred_element_type=jnp.float32)
    log_section = (mean_rate[:, :, None, :] + mixed).astype(jnp.bfloat16)
    rates = jnp.exp(log_section.astype(jnp.float32))
    onehot = (region_of == jnp.arange(REGIONS, dtype=jnp.int32)[None, :]).astype(jnp.float32)
    totals = jnp.einsum("sal,lg->sag", population, onehot, precision=highest)
    weighted = jnp.einsum(
        "sarl,lg->sarg", population[:, :, None, :] * rates, onehot, precision=highest
    )
    region_section = survival(weighted / totals[:, :, None, :])
    region_moved = lax.all_to_all(region_section, "loc", split_axis=2, concat_axis=1, tiled=True)
    region_survival = jnp.transpose(region_moved, (0, 2, 1))
    turned = jnp.transpose(
        lax.all_to_all(log_section, "loc", split_axis=3, concat_axis=2, tiled=True), (0, 1, 3, 2)
    )
    loc_survival = survival(jnp.exp(turned.astype(jnp.float32)))
    return (turned, loc_survival, region_survival)


def tie(x, other):
    return lax.optimization_barrier((x, other))


def split_bf16(x):
    hi = x.astype(jnp.bfloat16)
    return hi, (x - hi.astype(jnp.float32)).astype(jnp.bfloat16)


def age_mix_kernel(age_ref, x_ref, o_ref, done_ref, wide_ref):
    ages = age_ref.shape[0]
    rows = x_ref.shape[1]
    step = 256

    @pl.when(jnp.logical_and(pl.program_id(0) == 0, pl.program_id(1) == 0))
    def _():
        pick = lax.broadcasted_iota(jnp.int32, (rows, ages), 0) >> 4
        pick = (pick == lax.broadcasted_iota(jnp.int32, (rows, ages), 1)).astype(jnp.bfloat16)
        tall = jnp.dot(pick, age_ref[...], preferred_element_type=jnp.float32).astype(jnp.bfloat16)
        spread = lax.broadcasted_iota(jnp.int32, (ages, rows), 1) >> 4
        spread = (spread == lax.broadcasted_iota(jnp.int32, (ages, rows), 0)).astype(jnp.bfloat16)
        for lo in range(0, rows, step):
            hi = min(lo + step, rows)
            both = jnp.dot(tall[lo:hi], spread[:, :hi], preferred_element_type=jnp.float32)
            same = (lax.broadcasted_iota(jnp.int32, both.shape, 0) & 15) == (
                lax.broadcasted_iota(jnp.int32, both.shape, 1) & 15
            )
            wide_ref[lo:hi, :hi] = jnp.where(same, both, 0.0).astype(jnp.bfloat16)

    done_ref[...] = jnp.zeros_like(done_ref)
    for lo in range(0, rows, step):
        hi = min(lo + step, rows)
        o_ref[0, lo:hi, :] = jnp.dot(
            wide_ref[lo:hi, :hi], x_ref[0, :hi, :], preferred_element_type=jnp.float32
        ).astype(jnp.bfloat16)


def age_mix(age_factor, noise):
    sexes, rows, cols = noise.shape
    ages = age_factor.shape[0]
    width = 512
    return pl.pallas_call(
        age_mix_kernel,
        out_shape=(jax.ShapeDtypeStruct(noise.shape, jnp.bfloat16), jax.ShapeDtypeStruct((8, LANES), jnp.float32)),
        grid=(sexes, cols // width),
        in_specs=[
            pl.BlockSpec((ages, ages), lambda s, k: (0, 0)),
            pl.BlockSpec((1, rows, width), lambda s, k: (s, 0, k)),
        ],
        out_specs=(pl.BlockSpec((1, rows, width), lambda s, k: (s, 0, k)), pl.BlockSpec((8, LANES), lambda s, k: (0, 0))),
        scratch_shapes=[pltpu.VMEM((rows, rows), jnp.bfloat16)],
        compiler_params=pltpu.CompilerParams(vmem_limit_bytes=57 << 20),
        cost_estimate=pl.CostEstimate(
            flops=rows * rows * cols * sexes, bytes_accessed=4 * sexes * rows * cols, transcendentals=0
        ),
        name="age_mix",
    )(age_factor, noise)


def merge_pair(pair, odd_device, swapped):
    axis = pair.ndim - 1
    turned = pltpu.roll(pair, HALF, axis)
    first = jnp.where(odd_device, turned, pair)
    second = jnp.where(odd_device, pair, turned)
    low = lax.broadcasted_iota(jnp.int32, pair.shape[:-2] + (1, LANES), axis) < HALF
    s = 1 if swapped else 0
    return jnp.where(low, first[..., s : s + 1, :], second[..., 1 - s : 2 - s, :])


def loc_mix_kernel(bits, blocks, d_ref, x_ref, *refs):
    factors, refs = refs[:blocks], refs[blocks:]
    means, outs, done_ref = refs[:4], refs[5:9], refs[9]
    if blocks > 1:
        for i, f in enumerate(factors):
            refs[10][i * HALF : (i + 1) * HALF, :] = f[...]
    done_ref[...] = jnp.zeros_like(done_ref)
    if blocks == 1:
        parts = [factors[0][i * HALF : (i + 1) * HALF, :] for i in range(4)]
    else:
        parts = [f[...] for f in factors]
    ages, rows, _ = outs[0].shape
    sums = []
    for s, order in enumerate(((0, 1, 2, 3), (1, 0, 3, 2))):
        factor = jnp.concatenate([parts[i] for i in order], 0)
        sums.append(lax.dot_general(x_ref[s], factor, NT, preferred_element_type=jnp.float32))
    low = lax.broadcasted_iota(jnp.int32, (1, LANES), 1) < HALF
    for q in range(4):
        g = (q // 2) * LANES
        a, b = [x[:, g : g + LANES] for x in sums]
        v = jnp.where(low, a, b) if q % 2 == 0 else jnp.where(low, b, a)
        m = merge_pair(means[q][...], ((d_ref[0] ^ bits[q]) & 1) == 1, q % 2 == 1)
        outs[q][...] = (v.reshape(ages, rows, LANES) + m).astype(jnp.bfloat16)


def loc_mix(device, bits, mixed, factors, mean_t, done):
    sexes, rows, cols = mixed.shape
    ages = mean_t.shape[0]
    steps = 3
    block = ages // steps
    per_age = rows // ages
    msg = jax.ShapeDtypeStruct((ages, per_age, LANES), jnp.bfloat16)
    flag_spec = pl.BlockSpec(done.shape, lambda i, d: (0, 0))

    def mean_spec(q):
        return pl.BlockSpec((block, sexes, LANES), lambda i, d: (i, 0, (d[0] ^ bits[q]) // 2))

    outs = [msg] * 4 + [jax.ShapeDtypeStruct(done.shape, done.dtype)]
    out_specs = [pl.BlockSpec((block, per_age, LANES), lambda i, d: (i, 0, 0))] * 4 + [flag_spec]
    if len(factors) > 1:
        outs.append(jax.ShapeDtypeStruct((4 * HALF, cols), jnp.bfloat16))
        out_specs.append(pl.BlockSpec((4 * HALF, cols), lambda i, d: (0, 0)))
    return pl.pallas_call(
        functools.partial(loc_mix_kernel, bits, len(factors)),
        out_shape=outs,
        grid_spec=pltpu.PrefetchScalarGridSpec(
            num_scalar_prefetch=1,
            grid=(steps,),
            in_specs=[pl.BlockSpec((sexes, block * per_age, cols), lambda i, d: (0, i, 0))]
            + [pl.BlockSpec(f.shape, lambda i, d: (0, 0)) for f in factors]
            + [mean_spec(q) for q in range(4)]
            + [flag_spec],
            out_specs=out_specs,
        ),
        compiler_params=pltpu.CompilerParams(vmem_limit_bytes=57 << 20),
        cost_estimate=pl.CostEstimate(
            flops=2 * sexes * rows * cols * 256,
            bytes_accessed=2 * sexes * rows * cols + 8 * rows * LANES,
            transcendentals=0,
        ),
        name="loc_mix",
    )(device, mixed, *factors, *([mean_t] * 4), done)


def survive_kernel(bits, first, last, d_ref, *refs):
    xs, pops, regs = refs[:4], refs[4:8], refs[8:12]
    pos = 12
    if not first:
        locs_in, wsum_in, psum_in = refs[pos : pos + 3]
        pos += 3
    locs = refs[pos]
    pos += 1
    if not first:
        locs[...] = locs_in[...]
    if last:
        region_ref = refs[pos]
        pos += 1
    wsum_ref, psum_ref = refs[pos : pos + 2]
    hi_ref, lo_ref, pop_ref = refs[pos + 2 : pos + 5]
    ages, rows, _ = xs[0].shape
    dests = [d_ref[0] ^ b for b in bits]
    odd = [(e & 1) == 1 for e in dests]
    zero = jnp.zeros((rows, LANES), jnp.float32)

    def age_step(a, carry):
        hazards, totals = carry
        new_h, new_t = [], []
        at = pl.ds(pl.multiple_of(a * rows, rows), rows)
        for q in range(4):
            lanes = slice(q * LANES, (q + 1) * LANES)
            rate = jnp.exp(xs[q][a].astype(jnp.float32))
            h = hazards[q] + rate
            new_h.append(h)
            new_t.append(totals[q] + jnp.exp(-h))
            pop = merge_pair(pops[q][a], odd[q], q % 2 == 1)
            pop_ref[q, pl.ds(a, 1), :] = pop
            hi, lo = split_bf16(rate * pop)
            hi_ref[at, lanes] = hi
            lo_ref[at, lanes] = lo
        return tuple(new_h), tuple(new_t)

    hazards, totals = lax.fori_loop(0, ages, age_step, ((zero,) * 4, (zero,) * 4), unroll=3)
    for q in range(4):
        out = (totals[q] + (0.5 - 0.5 * jnp.exp(-hazards[q]))) * (1.0 / ages)
        if q % 2 == 1:
            out = pltpu.roll(out, HALF, 1)
        locs[dests[q]] = out

    lane = lax.broadcasted_iota(jnp.int32, (1, LANES), 1)
    low = lane < HALF
    onehots = []
    for q in range(4):
        pair = regs[q][...]
        turned = pltpu.roll(pair, HALF, 1)
        mine = jnp.where(low, jnp.where(odd[q], turned, pair), jnp.where(odd[q], pair, turned))
        upper = low if q % 2 == 1 else jnp.logical_not(low)
        target = mine + jnp.where(upper, REGIONS, 0)
        region = lax.broadcasted_iota(jnp.int32, (LANES, LANES), 0)
        onehots.append(jnp.where(region == target, 1.0, 0.0).astype(jnp.bfloat16))
    onehot = jnp.concatenate(onehots, 1)

    def regions(x):
        return lax.dot_general(x, onehot, NT, preferred_element_type=jnp.float32)

    pop_hi, pop_lo = split_bf16(jnp.concatenate([pop_ref[q] for q in range(4)], 1))
    wsum = regions(hi_ref[...]) + regions(lo_ref[...])
    psum = regions(pop_hi) + regions(pop_lo)
    if not first:
        wsum = wsum + wsum_in[...]
        psum = psum + psum_in[...]
    wsum_ref[...] = wsum
    psum_ref[...] = psum
    if last:

        def region_step(a, carry):
            h, t = carry
            at = pl.ds(pl.multiple_of(a * rows, rows), rows)
            h = h + wsum_ref[at, :] / psum_ref[pl.ds(a, 1), :]
            return h, t + jnp.exp(-h)

        h, t = lax.fori_loop(0, ages, region_step, (zero, zero), unroll=3)
        region_ref[...] = (t + (0.5 - 0.5 * jnp.exp(-h))) * (1.0 / ages)


def survive(device, bits, messages, pop_t, region_row, sums, last):
    ages, rows, _ = messages[0].shape
    sexes, locs = pop_t.shape[1], pop_t.shape[2] // HALF
    first = sums is None
    f32 = jnp.float32
    loc = jax.ShapeDtypeStruct((locs, rows, LANES), f32)
    wsum = jax.ShapeDtypeStruct((ages * rows, LANES), f32)
    psum = jax.ShapeDtypeStruct((ages, LANES), f32)
    whole = lambda *shape: pl.BlockSpec(shape, lambda i, d: (0,) * len(shape))

    def pop_spec(q):
        return pl.BlockSpec((ages, sexes, LANES), lambda i, d: (0, 0, (d[0] ^ bits[q]) // 2))

    def region_spec(q):
        return pl.BlockSpec((1, LANES), lambda i, d: (0, (d[0] ^ bits[q]) // 2))

    in_specs = [whole(ages, rows, LANES)] * 4
    in_specs += [pop_spec(q) for q in range(4)] + [region_spec(q) for q in range(4)]
    args = list(messages) + [pop_t] * 4 + [region_row] * 4
    sum_specs = [whole(ages * rows, LANES), whole(ages, LANES)]
    outs, out_specs = [loc], [whole(locs, rows, LANES)]
    if not first:
        in_specs += out_specs + sum_specs
        args += list(sums)
    if last:
        outs.append(jax.ShapeDtypeStruct((rows, LANES), f32))
        out_specs.append(whole(rows, LANES))
    scratch = [
        pltpu.VMEM((ages * rows, 4 * LANES), jnp.bfloat16),
        pltpu.VMEM((ages * rows, 4 * LANES), jnp.bfloat16),
        pltpu.VMEM((4, ages, LANES), f32),
    ]
    if last:
        scratch = [pltpu.VMEM(wsum.shape, f32), pltpu.VMEM(psum.shape, f32)] + scratch
    else:
        outs += [wsum, psum]
        out_specs += sum_specs
    return pl.pallas_call(
        functools.partial(survive_kernel, bits, first, last),
        out_shape=outs,
        grid_spec=pltpu.PrefetchScalarGridSpec(
            num_scalar_prefetch=1,
            grid=(1,),
            in_specs=in_specs,
            out_specs=out_specs,
            scratch_shapes=scratch,
        ),
        compiler_params=pltpu.CompilerParams(vmem_limit_bytes=57 << 20),
        cost_estimate=pl.CostEstimate(
            flops=60 * 4 * ages * rows * LANES,
            bytes_accessed=16 * ages * rows * LANES,
            transcendentals=8 * ages * rows * LANES,
        ),
        name="survive",
    )(device, *args)


def turn_kernel(near, d_ref, *refs):
    xs, out_ref, order_ref = refs[:8], refs[-2], refs[-1]
    d = d_ref[0]
    ages = xs[0].shape[0]
    for m in range(8):
        order_ref[(d & 7) ^ m] = xs[m][...]
    upper = (lax.broadcasted_iota(jnp.int32, (HALF, LANES), 1) >= HALF).astype(jnp.int32)
    swapped = (upper ^ ((d >> 2) & 1) ^ (1 if near else 0)) == 1
    for a in range(ages):
        tile = order_ref[:, a].reshape(LANES, LANES)
        t = tile.T.astype(jnp.float32)
        top, bottom = t[:HALF], t[HALF:]
        out_ref[0, a] = jnp.where(swapped, bottom, top).astype(jnp.bfloat16)
        out_ref[1, a] = jnp.where(swapped, top, bottom).astype(jnp.bfloat16)


def turn(device, messages, out_shape, previous, ready=()):
    near = previous is None
    ages, rows, _ = messages[0].shape
    steps = 3
    block = ages // steps
    in_specs = [pl.BlockSpec((block, rows, LANES), lambda i, d: (i, 0, 0))] * 8
    args = list(messages)
    flip = 0 if near else 1
    aliases = {}
    if not near:
        in_specs += [pl.BlockSpec(memory_space=pl.ANY)] * (1 + len(ready))
        args += [previous, *ready]
        aliases = {9: 0}
    return pl.pallas_call(
        functools.partial(turn_kernel, near),
        out_shape=out_shape,
        grid_spec=pltpu.PrefetchScalarGridSpec(
            num_scalar_prefetch=1,
            grid=(steps,),
            in_specs=in_specs,
            out_specs=pl.BlockSpec((2, block, HALF, LANES), lambda i, d: (0, i, 0, (d[0] // 8) ^ flip)),
            scratch_shapes=[pltpu.VMEM((8, block, rows, LANES), jnp.bfloat16)],
        ),
        input_output_aliases=aliases,
        compiler_params=pltpu.CompilerParams(vmem_limit_bytes=24 << 20),
        cost_estimate=pl.CostEstimate(
            flops=2 * ages * LANES**3, bytes_accessed=32 * ages * rows * LANES, transcendentals=0
        ),
        name="turn",
    )(device, *args)


def exchange(by_device, region_part, sexes):
    devices, rows, _ = by_device.shape
    mine = REGIONS // devices
    region_out = region_part.reshape(rows, sexes, devices, mine)
    region_out = jnp.transpose(region_out, (2, 1, 3, 0)).reshape(devices, 1, sexes * mine * rows)
    packed = jnp.concatenate([by_device, region_out], axis=1)
    small = lax.all_to_all(packed, "loc", split_axis=0, concat_axis=0, tiled=True)
    loc_survival = jnp.transpose(small[:, :rows].reshape(devices * rows, LANES), (1, 0))
    region_survival = jnp.transpose(
        small[:, rows].reshape(devices, sexes, mine, rows), (1, 2, 0, 3)
    ).reshape(sexes, mine, devices * rows)
    return loc_survival.reshape(sexes, HALF, devices * rows), region_survival


def shards_sixteen(noise, loc_factor, age_factor, mean_rate, population, region_of):
    sexes, ages, rows, locs = noise.shape
    devices = lax.axis_size("loc")
    here = lax.axis_index("loc")

    def swap(x, bits):
        return lax.ppermute(x, "loc", [(i, i ^ bits) for i in range(devices)])

    mean_t = jnp.transpose(mean_rate, (1, 0, 2))
    pop_t = jnp.transpose(population, (1, 0, 2))
    region_row = region_of.reshape(1, locs)
    device = here[None]

    factors = {0: loc_factor}
    for bits in (8, 12, 4):
        factors[bits] = swap(loc_factor, bits)
    mixed, done = age_mix(age_factor, noise.reshape(sexes, ages * rows, locs))
    factors, done = tie(factors, done)

    sent = {}

    def mix(c, lane, done):
        out = loc_mix(device, CHUNKS[c], mixed, lane, mean_t, done)
        sent.update(zip(CHUNKS[c], out[:4]))
        return out[4:]

    done, lane0 = mix(0, [factors[b] for b in CHUNKS[0]], done)
    lane1, done = tie(swap(lane0, 1), done)
    lane2, done = tie(swap(lane0, 2), done)
    (done,) = mix(1, [lane1], done)
    (done,) = mix(2, [lane2], done)
    lane3, done = tie(swap(lane2, 1), done)
    mix(3, [lane3], done)

    got = {0: sent[0]}
    first, sent[CHUNKS[3][3]] = tie(sent[CHUNKS[0][0]], sent[CHUNKS[3][3]])
    sums = None
    for i, b in enumerate(FAR):
        message = sent[b]
        if i >= 3:
            message, got[FAR[i - 3]] = tie(message, got[FAR[i - 3]])
        if i >= 4:
            bits = CHUNKS[i - 4]
            messages = [first if b == CHUNKS[0][0] else sent[b] for b in bits]
            sums = survive(device, bits, messages, pop_t, region_row, sums, i == 7)
            message, sums = tie(message, sums)
        got[b] = swap(message, b)
    for i, b in enumerate(NEAR):
        message = sent[b]
        if i >= 2:
            message, got[NEAR[i - 2]] = tie(message, got[NEAR[i - 2]])
        got[b] = swap(message, b)

    shape = jax.ShapeDtypeStruct((sexes, ages, HALF, devices * rows), jnp.bfloat16)
    close = [got[b] for b in range(8)]
    half = turn(device, close, shape, None)
    loc_survival, region_survival = exchange(*sums, sexes)
    ready = (loc_survival, region_survival)
    log_rates = turn(device, [got[b] for b in range(8, 16)], shape, half, ready)
    return (log_rates, loc_survival, region_survival)


def shards(noise, loc_factor, *rest):
    sixteen = lax.axis_size("loc") == 16 and noise.shape[2] == 16 and noise.shape[1] % 3 == 0
    if sixteen and noise.shape[0] == 2 and loc_factor.shape == (HALF, 1024):
        return shards_sixteen(noise, loc_factor, *rest)
    return shards_any(noise, loc_factor, *rest)


def solution(mesh):
    placed = (
        P(None, None, ("yr", "loc"), None),
        P("loc", None),
        P(),
        P("yr", None, None),
        P("yr", None, None),
        P(),
    )
    return jax.shard_map(
        shards,
        mesh=mesh,
        in_specs=placed,
        out_specs=(P(None, None, "loc", "yr"), P(None, "loc", "yr"), P(None, "loc", "yr")),
        check_vma=False,
    )
```

```python
import functools

import jax
import jax.numpy as jnp
from jax import lax
from jax.experimental import pallas as pl
from jax.experimental.pallas import tpu as pltpu
from jax.sharding import PartitionSpec as P

REGIONS = 64
LANES = 128
HALF = 64
NT = (((1,), (1,)), ((), ()))
CHUNKS = ((8, 12, 4, 0), (9, 13, 5, 1), (10, 14, 6, 2), (11, 15, 7, 3))
FAR = (8, 12, 9, 13, 10, 14, 11, 15)
NEAR = (4, 5, 1, 6, 2, 7, 3)
LONG = pl.CostEstimate(flops=20_000_000_000, bytes_accessed=1000, transcendentals=0)


def survival(rates):
    hazard = jnp.cumsum(rates, axis=1)
    after = jnp.exp(-hazard)
    total = 0.5 + jnp.sum(after, axis=1) - 0.5 * after[:, -1]
    return total / rates.shape[1]


def shards_any(noise, loc_factor, age_factor, mean_rate, population, region_of):
    highest = lax.Precision.HIGHEST
    spread = jnp.einsum(
        "sark,lk->sarl",
        noise,
        lax.all_gather(loc_factor, "loc", axis=0, tiled=True),
        preferred_element_type=jnp.float32,
    ).astype(jnp.bfloat16)
    mixed = jnp.einsum("ab,sbrl->sarl", age_factor, spread, preferred_element_type=jnp.float32)
    log_section = (mean_rate[:, :, None, :] + mixed).astype(jnp.bfloat16)
    rates = jnp.exp(log_section.astype(jnp.float32))
    onehot = (region_of == jnp.arange(REGIONS, dtype=jnp.int32)[None, :]).astype(jnp.float32)
    totals = jnp.einsum("sal,lg->sag", population, onehot, precision=highest)
    weighted = jnp.einsum(
        "sarl,lg->sarg", population[:, :, None, :] * rates, onehot, precision=highest
    )
    region_section = survival(weighted / totals[:, :, None, :])
    region_moved = lax.all_to_all(region_section, "loc", split_axis=2, concat_axis=1, tiled=True)
    region_survival = jnp.transpose(region_moved, (0, 2, 1))
    turned = jnp.transpose(
        lax.all_to_all(log_section, "loc", split_axis=3, concat_axis=2, tiled=True), (0, 1, 3, 2)
    )
    loc_survival = survival(jnp.exp(turned.astype(jnp.float32)))
    return (turned, loc_survival, region_survival)


def tie(x, other):
    return lax.optimization_barrier((x, other))


def split_bf16(x):
    hi = x.astype(jnp.bfloat16)
    return hi, (x - hi.astype(jnp.float32)).astype(jnp.bfloat16)


def age_mix_kernel(age_ref, x_ref, o_ref, done_ref, wide_ref):
    ages = age_ref.shape[0]
    rows = x_ref.shape[1]
    step = 256

    @pl.when(jnp.logical_and(pl.program_id(0) == 0, pl.program_id(1) == 0))
    def _():
        pick = lax.broadcasted_iota(jnp.int32, (rows, ages), 0) >> 4
        pick = (pick == lax.broadcasted_iota(jnp.int32, (rows, ages), 1)).astype(jnp.bfloat16)
        tall = jnp.dot(pick, age_ref[...], preferred_element_type=jnp.float32).astype(jnp.bfloat16)
        spread = lax.broadcasted_iota(jnp.int32, (ages, rows), 1) >> 4
        spread = (spread == lax.broadcasted_iota(jnp.int32, (ages, rows), 0)).astype(jnp.bfloat16)
        for lo in range(0, rows, step):
            hi = min(lo + step, rows)
            both = jnp.dot(tall[lo:hi], spread[:, :hi], preferred_element_type=jnp.float32)
            same = (lax.broadcasted_iota(jnp.int32, both.shape, 0) & 15) == (
                lax.broadcasted_iota(jnp.int32, both.shape, 1) & 15
            )
            wide_ref[lo:hi, :hi] = jnp.where(same, both, 0.0).astype(jnp.bfloat16)

    done_ref[...] = jnp.zeros_like(done_ref)
    for lo in range(0, rows, step):
        hi = min(lo + step, rows)
        o_ref[0, lo:hi, :] = jnp.dot(
            wide_ref[lo:hi, :hi], x_ref[0, :hi, :], preferred_element_type=jnp.float32
        ).astype(jnp.bfloat16)


def age_mix(age_factor, noise):
    sexes, rows, cols = noise.shape
    ages = age_factor.shape[0]
    width = 512
    return pl.pallas_call(
        age_mix_kernel,
        out_shape=(jax.ShapeDtypeStruct(noise.shape, jnp.bfloat16), jax.ShapeDtypeStruct((8, LANES), jnp.float32)),
        grid=(sexes, cols // width),
        in_specs=[
            pl.BlockSpec((ages, ages), lambda s, k: (0, 0)),
            pl.BlockSpec((1, rows, width), lambda s, k: (s, 0, k)),
        ],
        out_specs=(pl.BlockSpec((1, rows, width), lambda s, k: (s, 0, k)), pl.BlockSpec((8, LANES), lambda s, k: (0, 0))),
        scratch_shapes=[pltpu.VMEM((rows, rows), jnp.bfloat16)],
        compiler_params=pltpu.CompilerParams(vmem_limit_bytes=57 << 20),
        cost_estimate=LONG,
        name="age_mix",
    )(age_factor, noise)


def merge_pair(pair, odd_device, swapped):
    axis = pair.ndim - 1
    turned = pltpu.roll(pair, HALF, axis)
    first = jnp.where(odd_device, turned, pair)
    second = jnp.where(odd_device, pair, turned)
    low = lax.broadcasted_iota(jnp.int32, pair.shape[:-2] + (1, LANES), axis) < HALF
    s = 1 if swapped else 0
    return jnp.where(low, first[..., s : s + 1, :], second[..., 1 - s : 2 - s, :])


def loc_mix_kernel(groups, blocks, d_ref, x_ref, *refs):
    factors, refs = refs[:blocks], refs[blocks:]
    count = 4 * len(groups)
    means, outs, done_ref = refs[:count], refs[count + 1 : 2 * count + 1], refs[2 * count + 1]
    done_ref[...] = jnp.zeros_like(done_ref)
    if blocks > len(groups):
        joined_ref = refs[2 * count + 2]
        for i, f in enumerate(factors):
            joined_ref[i * HALF : (i + 1) * HALF, :] = f[...]
        factors = (joined_ref,)
    ages, rows, _ = outs[0].shape
    low = lax.broadcasted_iota(jnp.int32, (1, LANES), 1) < HALF
    for c, bits in enumerate(groups):
        parts = [factors[c][i * HALF : (i + 1) * HALF, :] for i in range(4)]
        sums = []
        for s, order in enumerate(((0, 1, 2, 3), (1, 0, 3, 2))):
            factor = jnp.concatenate([parts[i] for i in order], 0)
            sums.append(lax.dot_general(x_ref[s], factor, NT, preferred_element_type=jnp.float32))
        for q in range(4):
            g = (q // 2) * LANES
            a, b = [x[:, g : g + LANES] for x in sums]
            v = jnp.where(low, a, b) if q % 2 == 0 else jnp.where(low, b, a)
            at = 4 * c + q
            m = merge_pair(means[at][...], ((d_ref[0] ^ bits[q]) & 1) == 1, q % 2 == 1)
            outs[at][...] = (v.reshape(ages, rows, LANES) + m).astype(jnp.bfloat16)


def loc_mix(device, groups, mixed, factors, mean_t, done):
    sexes, rows, cols = mixed.shape
    ages = mean_t.shape[0]
    steps = 3
    block = ages // steps
    per_age = rows // ages
    every = [b for bits in groups for b in bits]
    msg = pltpu.HBM((ages, per_age, LANES), jnp.bfloat16)
    flag_spec = pl.BlockSpec(done.shape, lambda i, d: (0, 0))

    def mean_spec(b):
        return pl.BlockSpec((block, sexes, LANES), lambda i, d: (i, 0, (d[0] ^ b) // 2))

    outs = [msg] * len(every) + [jax.ShapeDtypeStruct(done.shape, done.dtype)]
    out_specs = [pl.BlockSpec((block, per_age, LANES), lambda i, d: (i, 0, 0))] * len(every) + [flag_spec]
    if len(factors) > len(groups):
        outs.append(jax.ShapeDtypeStruct((4 * HALF, cols), jnp.bfloat16))
        out_specs.append(pl.BlockSpec((4 * HALF, cols), lambda i, d: (0, 0)))
    return pl.pallas_call(
        functools.partial(loc_mix_kernel, groups, len(factors)),
        out_shape=outs,
        grid_spec=pltpu.PrefetchScalarGridSpec(
            num_scalar_prefetch=1,
            grid=(steps,),
            in_specs=[pl.BlockSpec((sexes, block * per_age, cols), lambda i, d: (0, i, 0))]
            + [pl.BlockSpec(f.shape, lambda i, d: (0, 0)) for f in factors]
            + [mean_spec(b) for b in every]
            + [flag_spec],
            out_specs=out_specs,
        ),
        compiler_params=pltpu.CompilerParams(vmem_limit_bytes=57 << 20),
        cost_estimate=LONG,
        name="loc_mix",
    )(device, mixed, *factors, *([mean_t] * len(every)), done)


def survive_kernel(d_ref, *refs):
    count = 4 * len(CHUNKS)
    xs, pops, regs = refs[:count], refs[count : 2 * count], refs[2 * count : 3 * count]
    locs, region_ref, hi_ref, lo_ref, pop_ref, wsum_ref, psum_ref = refs[3 * count :]
    ages, rows, _ = xs[0].shape
    zero = jnp.zeros((rows, LANES), jnp.float32)
    lane = lax.broadcasted_iota(jnp.int32, (1, LANES), 1)
    low = lane < HALF
    for c, bits in enumerate(CHUNKS):
        dests = [d_ref[0] ^ b for b in bits]
        odd = [(e & 1) == 1 for e in dests]
        first = 4 * c

        def age_step(a, carry):
            hazards, totals = carry
            new_h, new_t = [], []
            at = pl.ds(pl.multiple_of(a * rows, rows), rows)
            for q in range(4):
                lanes = slice(q * LANES, (q + 1) * LANES)
                rate = jnp.exp(xs[first + q][a].astype(jnp.float32))
                h = hazards[q] + rate
                new_h.append(h)
                new_t.append(totals[q] + jnp.exp(-h))
                pop = merge_pair(pops[first + q][a], odd[q], q % 2 == 1)
                pop_ref[q, pl.ds(a, 1), :] = pop
                hi, lo = split_bf16(rate * pop)
                hi_ref[at, lanes] = hi
                lo_ref[at, lanes] = lo
            return tuple(new_h), tuple(new_t)

        hazards, totals = lax.fori_loop(0, ages, age_step, ((zero,) * 4, (zero,) * 4), unroll=3)
        onehots = []
        for q in range(4):
            out = (totals[q] + (0.5 - 0.5 * jnp.exp(-hazards[q]))) * (1.0 / ages)
            if q % 2 == 1:
                out = pltpu.roll(out, HALF, 1)
            locs[dests[q]] = out
            pair = regs[first + q][...]
            turned = pltpu.roll(pair, HALF, 1)
            mine = jnp.where(low, jnp.where(odd[q], turned, pair), jnp.where(odd[q], pair, turned))
            upper = low if q % 2 == 1 else jnp.logical_not(low)
            target = mine + jnp.where(upper, REGIONS, 0)
            region = lax.broadcasted_iota(jnp.int32, (LANES, LANES), 0)
            onehots.append(jnp.where(region == target, 1.0, 0.0).astype(jnp.bfloat16))
        onehot = jnp.concatenate(onehots, 1)

        def regions(x):
            return lax.dot_general(x, onehot, NT, preferred_element_type=jnp.float32)

        pop_hi, pop_lo = split_bf16(jnp.concatenate([pop_ref[q] for q in range(4)], 1))
        wsum = regions(hi_ref[...]) + regions(lo_ref[...])
        psum = regions(pop_hi) + regions(pop_lo)
        if c > 0:
            wsum = wsum + wsum_ref[...]
            psum = psum + psum_ref[...]
        wsum_ref[...] = wsum
        psum_ref[...] = psum

    def region_step(a, carry):
        h, t = carry
        at = pl.ds(pl.multiple_of(a * rows, rows), rows)
        h = h + wsum_ref[at, :] / psum_ref[pl.ds(a, 1), :]
        return h, t + jnp.exp(-h)

    h, t = lax.fori_loop(0, ages, region_step, (zero, zero), unroll=3)
    region_ref[...] = (t + (0.5 - 0.5 * jnp.exp(-h))) * (1.0 / ages)


def survive(device, sent, pop_t, region_row):
    every = [b for bits in CHUNKS for b in bits]
    ages, rows, _ = sent[0].shape
    sexes, locs = pop_t.shape[1], pop_t.shape[2] // HALF
    f32 = jnp.float32
    whole = lambda *shape: pl.BlockSpec(shape, lambda i, d: (0,) * len(shape))

    def pop_spec(b):
        return pl.BlockSpec((ages, sexes, LANES), lambda i, d: (0, 0, (d[0] ^ b) // 2))

    def region_spec(b):
        return pl.BlockSpec((1, LANES), lambda i, d: (0, (d[0] ^ b) // 2))

    return pl.pallas_call(
        survive_kernel,
        out_shape=(
            jax.ShapeDtypeStruct((locs, rows, LANES), f32),
            jax.ShapeDtypeStruct((rows, LANES), f32),
        ),
        grid_spec=pltpu.PrefetchScalarGridSpec(
            num_scalar_prefetch=1,
            grid=(1,),
            in_specs=[whole(ages, rows, LANES)] * len(every)
            + [pop_spec(b) for b in every]
            + [region_spec(b) for b in every],
            out_specs=(whole(locs, rows, LANES), whole(rows, LANES)),
            scratch_shapes=[
                pltpu.VMEM((ages * rows, 4 * LANES), jnp.bfloat16),
                pltpu.VMEM((ages * rows, 4 * LANES), jnp.bfloat16),
                pltpu.VMEM((4, ages, LANES), f32),
                pltpu.VMEM((ages * rows, LANES), f32),
                pltpu.VMEM((ages, LANES), f32),
            ],
        ),
        compiler_params=pltpu.CompilerParams(vmem_limit_bytes=57 << 20),
        cost_estimate=LONG,
        name="survive",
    )(device, *[sent[b] for b in every], *([pop_t] * len(every)), *([region_row] * len(every)))


def turn_kernel(near, d_ref, *refs):
    xs, out_ref, order_ref = refs[:8], refs[-2], refs[-1]
    d = d_ref[0]
    ages = xs[0].shape[0]
    for m in range(8):
        order_ref[(d & 7) ^ m] = xs[m][...]
    upper = (lax.broadcasted_iota(jnp.int32, (HALF, LANES), 1) >= HALF).astype(jnp.int32)
    swapped = (upper ^ ((d >> 2) & 1) ^ (1 if near else 0)) == 1
    for a in range(ages):
        tile = order_ref[:, a].reshape(LANES, LANES)
        t = tile.T.astype(jnp.float32)
        top, bottom = t[:HALF], t[HALF:]
        out_ref[0, a] = jnp.where(swapped, bottom, top).astype(jnp.bfloat16)
        out_ref[1, a] = jnp.where(swapped, top, bottom).astype(jnp.bfloat16)


def turn(device, messages, out_shape, previous, ready=()):
    near = previous is None
    ages, rows, _ = messages[0].shape
    steps = 3
    block = ages // steps
    in_specs = [pl.BlockSpec((block, rows, LANES), lambda i, d: (i, 0, 0))] * 8
    args = list(messages)
    flip = 0 if near else 1
    aliases = {}
    if not near:
        in_specs += [pl.BlockSpec(memory_space=pl.ANY)] * (1 + len(ready))
        args += [previous, *ready]
        aliases = {9: 0}
    return pl.pallas_call(
        functools.partial(turn_kernel, near),
        out_shape=out_shape,
        grid_spec=pltpu.PrefetchScalarGridSpec(
            num_scalar_prefetch=1,
            grid=(steps,),
            in_specs=in_specs,
            out_specs=pl.BlockSpec((2, block, HALF, LANES), lambda i, d: (0, i, 0, (d[0] // 8) ^ flip)),
            scratch_shapes=[pltpu.VMEM((8, block, rows, LANES), jnp.bfloat16)],
        ),
        input_output_aliases=aliases,
        compiler_params=pltpu.CompilerParams(vmem_limit_bytes=(57 if near else 24) << 20),
        cost_estimate=LONG,
        name="turn",
    )(device, *args)


def exchange(by_device, region_part, sexes):
    devices, rows, _ = by_device.shape
    mine = REGIONS // devices
    region_out = region_part.reshape(rows, sexes, devices, mine)
    region_out = jnp.transpose(region_out, (2, 1, 3, 0)).reshape(devices, 1, sexes * mine * rows)
    packed = jnp.concatenate([by_device, region_out], axis=1)
    small = lax.all_to_all(packed, "loc", split_axis=0, concat_axis=0, tiled=True)
    loc_survival = jnp.transpose(small[:, :rows].reshape(devices * rows, LANES), (1, 0))
    region_survival = jnp.transpose(
        small[:, rows].reshape(devices, sexes, mine, rows), (1, 2, 0, 3)
    ).reshape(sexes, mine, devices * rows)
    return loc_survival.reshape(sexes, HALF, devices * rows), region_survival


def shards_sixteen(noise, loc_factor, age_factor, mean_rate, population, region_of):
    sexes, ages, rows, locs = noise.shape
    devices = lax.axis_size("loc")
    here = lax.axis_index("loc")

    def swap(x, bits):
        return lax.ppermute(x, "loc", [(i, i ^ bits) for i in range(devices)])

    mean_t = jnp.transpose(mean_rate, (1, 0, 2))
    pop_t = jnp.transpose(population, (1, 0, 2))
    region_row = region_of.reshape(1, locs)
    device = here[None]

    factors = {0: loc_factor}
    for bits in (8, 12, 4):
        factors[bits] = swap(loc_factor, bits)
    mixed, done = age_mix(age_factor, noise.reshape(sexes, ages * rows, locs))
    factors, done = tie(factors, done)

    sent = {}

    def mix(groups, lanes, done):
        out = loc_mix(device, groups, mixed, lanes, mean_t, done)
        count = 4 * len(groups)
        sent.update(zip([b for bits in groups for b in bits], out[:count]))
        return out[count:]

    done, lane0 = mix(CHUNKS[:1], [factors[b] for b in CHUNKS[0]], done)
    lanes = [swap(lane0, bits) for bits in (1, 2, 3)]
    (done,) = mix(CHUNKS[1:2], lanes[:1], done)
    lanes, done = tie(lanes, done)
    (done,) = mix(CHUNKS[2:], lanes[1:], done)

    got = {0: sent[0]}
    for i, b in enumerate(NEAR):
        message = sent[b]
        if i >= 2:
            message, got[NEAR[i - 2]] = tie(message, got[NEAR[i - 2]])
        got[b] = swap(message, b)
    sums = None
    for i, b in enumerate(FAR):
        message = sent[b]
        if i >= 2:
            ahead = FAR[max(i - 3, min(i - 2, 1))]
            message, got[ahead] = tie(message, got[ahead])
        if i == 5:
            sums = survive(device, sent, pop_t, region_row)
            message, sums = tie(message, sums)
        if i == 7:
            small = exchange(*sums, sexes)
            message, small = tie(message, small)
        got[b] = swap(message, b)

    shape = jax.ShapeDtypeStruct((sexes, ages, HALF, devices * rows), jnp.bfloat16)
    close = [got[b] for b in range(8)]
    half = turn(device, close, shape, None)
    loc_survival, region_survival = small
    ready = (loc_survival, region_survival)
    log_rates = turn(device, [got[b] for b in range(8, 16)], shape, half, ready)
    return (log_rates, loc_survival, region_survival)


def shards(noise, loc_factor, *rest):
    sixteen = lax.axis_size("loc") == 16 and noise.shape[2] == 16 and noise.shape[1] % 3 == 0
    if sixteen and noise.shape[0] == 2 and loc_factor.shape == (HALF, 1024):
        return shards_sixteen(noise, loc_factor, *rest)
    return shards_any(noise, loc_factor, *rest)


def solution(mesh):
    placed = (
        P(None, None, ("yr", "loc"), None),
        P("loc", None),
        P(),
        P("yr", None, None),
        P("yr", None, None),
        P(),
    )
    return jax.shard_map(
        shards,
        mesh=mesh,
        in_specs=placed,
        out_specs=(P(None, None, "loc", "yr"), P(None, "loc", "yr"), P(None, "loc", "yr")),
        check_vma=False,
    )
```

```python
import functools

import jax
import jax.numpy as jnp
from jax import lax
from jax.experimental import pallas as pl
from jax.experimental.pallas import tpu as pltpu
from jax.sharding import PartitionSpec as P

REGIONS = 64
LANES = 128
HALF = 64
NT = (((1,), (1,)), ((), ()))
CHUNKS = ((8, 12, 4, 0), (9, 13, 5, 1), (10, 14, 6, 2), (11, 15, 7, 3))
FAR = (8, 12, 9, 13, 10, 14, 11, 15)
NEAR = (4, 5, 1, 6, 2, 7, 3)
LONG = pl.CostEstimate(flops=20_000_000_000, bytes_accessed=1000, transcendentals=0)


def survival(rates):
    hazard = jnp.cumsum(rates, axis=1)
    after = jnp.exp(-hazard)
    total = 0.5 + jnp.sum(after, axis=1) - 0.5 * after[:, -1]
    return total / rates.shape[1]


def shards_any(noise, loc_factor, age_factor, mean_rate, population, region_of):
    highest = lax.Precision.HIGHEST
    spread = jnp.einsum(
        "sark,lk->sarl",
        noise,
        lax.all_gather(loc_factor, "loc", axis=0, tiled=True),
        preferred_element_type=jnp.float32,
    ).astype(jnp.bfloat16)
    mixed = jnp.einsum("ab,sbrl->sarl", age_factor, spread, preferred_element_type=jnp.float32)
    log_section = (mean_rate[:, :, None, :] + mixed).astype(jnp.bfloat16)
    rates = jnp.exp(log_section.astype(jnp.float32))
    onehot = (region_of == jnp.arange(REGIONS, dtype=jnp.int32)[None, :]).astype(jnp.float32)
    totals = jnp.einsum("sal,lg->sag", population, onehot, precision=highest)
    weighted = jnp.einsum(
        "sarl,lg->sarg", population[:, :, None, :] * rates, onehot, precision=highest
    )
    region_section = survival(weighted / totals[:, :, None, :])
    region_moved = lax.all_to_all(region_section, "loc", split_axis=2, concat_axis=1, tiled=True)
    region_survival = jnp.transpose(region_moved, (0, 2, 1))
    turned = jnp.transpose(
        lax.all_to_all(log_section, "loc", split_axis=3, concat_axis=2, tiled=True), (0, 1, 3, 2)
    )
    loc_survival = survival(jnp.exp(turned.astype(jnp.float32)))
    return (turned, loc_survival, region_survival)


def tie(x, other):
    return lax.optimization_barrier((x, other))


def split_bf16(x):
    hi = x.astype(jnp.bfloat16)
    return hi, (x - hi.astype(jnp.float32)).astype(jnp.bfloat16)


def age_mix_kernel(age_ref, x_ref, o_ref, done_ref, wide_ref):
    ages = age_ref.shape[0]
    rows = x_ref.shape[1]
    step = 256

    @pl.when(jnp.logical_and(pl.program_id(0) == 0, pl.program_id(1) == 0))
    def _():
        pick = lax.broadcasted_iota(jnp.int32, (rows, ages), 0) >> 4
        pick = (pick == lax.broadcasted_iota(jnp.int32, (rows, ages), 1)).astype(jnp.bfloat16)
        tall = jnp.dot(pick, age_ref[...], preferred_element_type=jnp.float32).astype(jnp.bfloat16)
        spread = lax.broadcasted_iota(jnp.int32, (ages, rows), 1) >> 4
        spread = (spread == lax.broadcasted_iota(jnp.int32, (ages, rows), 0)).astype(jnp.bfloat16)
        for lo in range(0, rows, step):
            hi = min(lo + step, rows)
            both = jnp.dot(tall[lo:hi], spread[:, :hi], preferred_element_type=jnp.float32)
            same = (lax.broadcasted_iota(jnp.int32, both.shape, 0) & 15) == (
                lax.broadcasted_iota(jnp.int32, both.shape, 1) & 15
            )
            wide_ref[lo:hi, :hi] = jnp.where(same, both, 0.0).astype(jnp.bfloat16)

    done_ref[...] = jnp.zeros_like(done_ref)
    for lo in range(0, rows, step):
        hi = min(lo + step, rows)
        o_ref[0, lo:hi, :] = jnp.dot(
            wide_ref[lo:hi, :hi], x_ref[0, :hi, :], preferred_element_type=jnp.float32
        ).astype(jnp.bfloat16)


def age_mix(age_factor, noise):
    sexes, rows, cols = noise.shape
    ages = age_factor.shape[0]
    width = 512
    return pl.pallas_call(
        age_mix_kernel,
        out_shape=(jax.ShapeDtypeStruct(noise.shape, jnp.bfloat16), jax.ShapeDtypeStruct((8, LANES), jnp.float32)),
        grid=(sexes, cols // width),
        in_specs=[
            pl.BlockSpec((ages, ages), lambda s, k: (0, 0)),
            pl.BlockSpec((1, rows, width), lambda s, k: (s, 0, k)),
        ],
        out_specs=(pl.BlockSpec((1, rows, width), lambda s, k: (s, 0, k)), pl.BlockSpec((8, LANES), lambda s, k: (0, 0))),
        scratch_shapes=[pltpu.VMEM((rows, rows), jnp.bfloat16)],
        compiler_params=pltpu.CompilerParams(vmem_limit_bytes=57 << 20),
        cost_estimate=LONG,
        name="age_mix",
    )(age_factor, noise)


def merge_pair(pair, odd_device, swapped):
    axis = pair.ndim - 1
    turned = pltpu.roll(pair, HALF, axis)
    first = jnp.where(odd_device, turned, pair)
    second = jnp.where(odd_device, pair, turned)
    low = lax.broadcasted_iota(jnp.int32, pair.shape[:-2] + (1, LANES), axis) < HALF
    s = 1 if swapped else 0
    return jnp.where(low, first[..., s : s + 1, :], second[..., 1 - s : 2 - s, :])


def loc_mix_kernel(groups, blocks, d_ref, x_ref, *refs):
    factors, refs = refs[:blocks], refs[blocks:]
    count = 4 * len(groups)
    means, outs, done_ref = refs[:count], refs[count + 1 : 2 * count + 1], refs[2 * count + 1]
    done_ref[...] = jnp.zeros_like(done_ref)
    if blocks > len(groups):
        joined_ref = refs[2 * count + 2]
        for i, f in enumerate(factors):
            joined_ref[i * HALF : (i + 1) * HALF, :] = f[...]
        factors = (joined_ref,)
    ages, rows, _ = outs[0].shape
    low = lax.broadcasted_iota(jnp.int32, (1, LANES), 1) < HALF
    for c, bits in enumerate(groups):
        parts = [factors[c][i * HALF : (i + 1) * HALF, :] for i in range(4)]
        sums = []
        for s, order in enumerate(((0, 1, 2, 3), (1, 0, 3, 2))):
            factor = jnp.concatenate([parts[i] for i in order], 0)
            sums.append(lax.dot_general(x_ref[s], factor, NT, preferred_element_type=jnp.float32))
        for q in range(4):
            g = (q // 2) * LANES
            a, b = [x[:, g : g + LANES] for x in sums]
            v = jnp.where(low, a, b) if q % 2 == 0 else jnp.where(low, b, a)
            at = 4 * c + q
            m = merge_pair(means[at][...], ((d_ref[0] ^ bits[q]) & 1) == 1, q % 2 == 1)
            outs[at][...] = (v.reshape(ages, rows, LANES) + m).astype(jnp.bfloat16)


def loc_mix(device, groups, mixed, factors, mean_t, done):
    sexes, rows, cols = mixed.shape
    ages = mean_t.shape[0]
    steps = 3
    block = ages // steps
    per_age = rows // ages
    every = [b for bits in groups for b in bits]
    msg = pltpu.HBM((ages, per_age, LANES), jnp.bfloat16)
    flag_spec = pl.BlockSpec(done.shape, lambda i, d: (0, 0))

    def mean_spec(b):
        return pl.BlockSpec((block, sexes, LANES), lambda i, d: (i, 0, (d[0] ^ b) // 2))

    outs = [msg] * len(every) + [jax.ShapeDtypeStruct(done.shape, done.dtype)]
    out_specs = [pl.BlockSpec((block, per_age, LANES), lambda i, d: (i, 0, 0))] * len(every) + [flag_spec]
    if len(factors) > len(groups):
        outs.append(jax.ShapeDtypeStruct((4 * HALF, cols), jnp.bfloat16))
        out_specs.append(pl.BlockSpec((4 * HALF, cols), lambda i, d: (0, 0)))
    return pl.pallas_call(
        functools.partial(loc_mix_kernel, groups, len(factors)),
        out_shape=outs,
        grid_spec=pltpu.PrefetchScalarGridSpec(
            num_scalar_prefetch=1,
            grid=(steps,),
            in_specs=[pl.BlockSpec((sexes, block * per_age, cols), lambda i, d: (0, i, 0))]
            + [pl.BlockSpec(f.shape, lambda i, d: (0, 0)) for f in factors]
            + [mean_spec(b) for b in every]
            + [flag_spec],
            out_specs=out_specs,
        ),
        compiler_params=pltpu.CompilerParams(vmem_limit_bytes=57 << 20),
        cost_estimate=LONG,
        name="loc_mix",
    )(device, mixed, *factors, *([mean_t] * len(every)), done)


def survive_kernel(d_ref, *refs):
    count = 4 * len(CHUNKS)
    xs, pops, regs = refs[:count], refs[count : 2 * count], refs[2 * count : 3 * count]
    locs, region_ref, hi_ref, lo_ref, pop_ref, wsum_ref, psum_ref = refs[3 * count + 1 :]
    ages, rows, _ = xs[0].shape
    zero = jnp.zeros((rows, LANES), jnp.float32)
    lane = lax.broadcasted_iota(jnp.int32, (1, LANES), 1)
    low = lane < HALF
    for c, bits in enumerate(CHUNKS):
        dests = [d_ref[0] ^ b for b in bits]
        odd = [(e & 1) == 1 for e in dests]
        first = 4 * c

        def age_step(a, carry):
            hazards, totals = carry
            new_h, new_t = [], []
            at = pl.ds(pl.multiple_of(a * rows, rows), rows)
            for q in range(4):
                lanes = slice(q * LANES, (q + 1) * LANES)
                rate = jnp.exp(xs[first + q][a].astype(jnp.float32))
                h = hazards[q] + rate
                new_h.append(h)
                new_t.append(totals[q] + jnp.exp(-h))
                pop = merge_pair(pops[first + q][a], odd[q], q % 2 == 1)
                pop_ref[q, pl.ds(a, 1), :] = pop
                hi, lo = split_bf16(rate * pop)
                hi_ref[at, lanes] = hi
                lo_ref[at, lanes] = lo
            return tuple(new_h), tuple(new_t)

        hazards, totals = lax.fori_loop(0, ages, age_step, ((zero,) * 4, (zero,) * 4), unroll=3)
        onehots = []
        for q in range(4):
            out = (totals[q] + (0.5 - 0.5 * jnp.exp(-hazards[q]))) * (1.0 / ages)
            if q % 2 == 1:
                out = pltpu.roll(out, HALF, 1)
            locs[dests[q]] = out
            pair = regs[first + q][...]
            turned = pltpu.roll(pair, HALF, 1)
            mine = jnp.where(low, jnp.where(odd[q], turned, pair), jnp.where(odd[q], pair, turned))
            upper = low if q % 2 == 1 else jnp.logical_not(low)
            target = mine + jnp.where(upper, REGIONS, 0)
            region = lax.broadcasted_iota(jnp.int32, (LANES, LANES), 0)
            onehots.append(jnp.where(region == target, 1.0, 0.0).astype(jnp.bfloat16))
        onehot = jnp.concatenate(onehots, 1)

        def regions(x):
            return lax.dot_general(x, onehot, NT, preferred_element_type=jnp.float32)

        pop_hi, pop_lo = split_bf16(jnp.concatenate([pop_ref[q] for q in range(4)], 1))
        wsum = regions(hi_ref[...]) + regions(lo_ref[...])
        psum = regions(pop_hi) + regions(pop_lo)
        if c > 0:
            wsum = wsum + wsum_ref[...]
            psum = psum + psum_ref[...]
        wsum_ref[...] = wsum
        psum_ref[...] = psum

    def region_step(a, carry):
        h, t = carry
        at = pl.ds(pl.multiple_of(a * rows, rows), rows)
        h = h + wsum_ref[at, :] / psum_ref[pl.ds(a, 1), :]
        return h, t + jnp.exp(-h)

    h, t = lax.fori_loop(0, ages, region_step, (zero, zero), unroll=3)
    region_ref[...] = (t + (0.5 - 0.5 * jnp.exp(-h))) * (1.0 / ages)


def survive(device, sent, pop_t, region_row, done):
    every = [b for bits in CHUNKS for b in bits]
    ages, rows, _ = sent[0].shape
    sexes, locs = pop_t.shape[1], pop_t.shape[2] // HALF
    f32 = jnp.float32
    whole = lambda *shape: pl.BlockSpec(shape, lambda i, d: (0,) * len(shape))

    def pop_spec(b):
        return pl.BlockSpec((ages, sexes, LANES), lambda i, d: (0, 0, (d[0] ^ b) // 2))

    def region_spec(b):
        return pl.BlockSpec((1, LANES), lambda i, d: (0, (d[0] ^ b) // 2))

    return pl.pallas_call(
        survive_kernel,
        out_shape=(
            jax.ShapeDtypeStruct((locs, rows, LANES), f32),
            jax.ShapeDtypeStruct((rows, LANES), f32),
        ),
        grid_spec=pltpu.PrefetchScalarGridSpec(
            num_scalar_prefetch=1,
            grid=(1,),
            in_specs=[whole(ages, rows, LANES)] * len(every)
            + [pop_spec(b) for b in every]
            + [region_spec(b) for b in every]
            + [whole(*done.shape)],
            out_specs=(whole(locs, rows, LANES), whole(rows, LANES)),
            scratch_shapes=[
                pltpu.VMEM((ages * rows, 4 * LANES), jnp.bfloat16),
                pltpu.VMEM((ages * rows, 4 * LANES), jnp.bfloat16),
                pltpu.VMEM((4, ages, LANES), f32),
                pltpu.VMEM((ages * rows, LANES), f32),
                pltpu.VMEM((ages, LANES), f32),
            ],
        ),
        compiler_params=pltpu.CompilerParams(vmem_limit_bytes=57 << 20),
        cost_estimate=LONG,
        name="survive",
    )(device, *[sent[b] for b in every], *([pop_t] * len(every)), *([region_row] * len(every)), done)


def turn_kernel(near, d_ref, *refs):
    xs, out_ref, order_ref = refs[:8], refs[-2], refs[-1]
    d = d_ref[0]
    ages = xs[0].shape[0]
    for m in range(8):
        order_ref[(d & 7) ^ m] = xs[m][...]
    upper = (lax.broadcasted_iota(jnp.int32, (HALF, LANES), 1) >= HALF).astype(jnp.int32)
    swapped = (upper ^ ((d >> 2) & 1) ^ (1 if near else 0)) == 1
    for a in range(ages):
        tile = order_ref[:, a].reshape(LANES, LANES)
        t = tile.T.astype(jnp.float32)
        top, bottom = t[:HALF], t[HALF:]
        out_ref[0, a] = jnp.where(swapped, bottom, top).astype(jnp.bfloat16)
        out_ref[1, a] = jnp.where(swapped, top, bottom).astype(jnp.bfloat16)


def turn(device, messages, out_shape, previous, ready=()):
    near = previous is None
    ages, rows, _ = messages[0].shape
    steps = 3
    block = ages // steps
    in_specs = [pl.BlockSpec((block, rows, LANES), lambda i, d: (i, 0, 0))] * 8
    args = list(messages)
    flip = 0 if near else 1
    aliases = {}
    if not near:
        in_specs += [pl.BlockSpec(memory_space=pl.ANY)] * (1 + len(ready))
        args += [previous, *ready]
        aliases = {9: 0}
    return pl.pallas_call(
        functools.partial(turn_kernel, near),
        out_shape=out_shape,
        grid_spec=pltpu.PrefetchScalarGridSpec(
            num_scalar_prefetch=1,
            grid=(steps,),
            in_specs=in_specs,
            out_specs=pl.BlockSpec((2, block, HALF, LANES), lambda i, d: (0, i, 0, (d[0] // 8) ^ flip)),
            scratch_shapes=[pltpu.VMEM((8, block, rows, LANES), jnp.bfloat16)],
        ),
        input_output_aliases=aliases,
        compiler_params=pltpu.CompilerParams(vmem_limit_bytes=(57 if near else 24) << 20),
        cost_estimate=LONG,
        name="turn",
    )(device, *args)


def exchange(by_device, region_part, sexes):
    devices, rows, _ = by_device.shape
    mine = REGIONS // devices
    region_out = region_part.reshape(rows, sexes, devices, mine)
    region_out = jnp.transpose(region_out, (2, 1, 3, 0)).reshape(devices, 1, sexes * mine * rows)
    packed = jnp.concatenate([by_device, region_out], axis=1)
    return lax.all_to_all(packed, "loc", split_axis=0, concat_axis=0, tiled=True)


def unpack(small, rows, sexes):
    devices = small.shape[0]
    mine = REGIONS // devices
    loc_survival = jnp.transpose(small[:, :rows].reshape(devices * rows, LANES), (1, 0))
    region_survival = jnp.transpose(
        small[:, rows].reshape(devices, sexes, mine, rows), (1, 2, 0, 3)
    ).reshape(sexes, mine, devices * rows)
    return loc_survival.reshape(sexes, HALF, devices * rows), region_survival


def shards_sixteen(noise, loc_factor, age_factor, mean_rate, population, region_of):
    sexes, ages, rows, locs = noise.shape
    devices = lax.axis_size("loc")
    here = lax.axis_index("loc")

    def swap(x, bits):
        return lax.ppermute(x, "loc", [(i, i ^ bits) for i in range(devices)])

    mean_t = jnp.transpose(mean_rate, (1, 0, 2))
    pop_t = jnp.transpose(population, (1, 0, 2))
    region_row = region_of.reshape(1, locs)
    device = here[None]

    factors = {0: loc_factor}
    for bits in (8, 12, 4):
        factors[bits] = swap(loc_factor, bits)
    mixed, done = age_mix(age_factor, noise.reshape(sexes, ages * rows, locs))
    factors, done = tie(factors, done)

    sent = {}

    def mix(groups, lanes, done):
        out = loc_mix(device, groups, mixed, lanes, mean_t, done)
        count = 4 * len(groups)
        sent.update(zip([b for bits in groups for b in bits], out[:count]))
        return out[count:]

    done, lane0 = mix(CHUNKS[:1], [factors[b] for b in CHUNKS[0]], done)
    lanes = [swap(lane0, bits) for bits in (1, 2, 3)]
    (done,) = mix(CHUNKS[1:2], lanes[:1], done)
    lanes, done = tie(lanes, done)
    (done,) = mix(CHUNKS[2:], lanes[1:], done)

    got = {0: sent[0]}
    for i, b in enumerate(NEAR):
        message = sent[b]
        if 0 < i < 3:
            message, done = tie(message, done)
        if i >= 2:
            message, got[NEAR[i - 2]] = tie(message, got[NEAR[i - 2]])
        got[b] = swap(message, b)
    sums = None
    for i, b in enumerate(FAR):
        message = sent[b]
        if i >= 2:
            ahead = FAR[max(i - 3, min(i - 2, 1))]
            message, got[ahead] = tie(message, got[ahead])
        if i == 5:
            sums = survive(device, sent, pop_t, region_row, done)
            small = exchange(*sums, sexes)
            message, small = tie(message, small)
        got[b] = swap(message, b)

    shape = jax.ShapeDtypeStruct((sexes, ages, HALF, devices * rows), jnp.bfloat16)
    close = [got[b] for b in range(8)]
    half = turn(device, close, shape, None)
    loc_survival, region_survival = unpack(small, rows, sexes)
    ready = (loc_survival, region_survival)
    log_rates = turn(device, [got[b] for b in range(8, 16)], shape, half, ready)
    return (log_rates, loc_survival, region_survival)


def shards(noise, loc_factor, *rest):
    sixteen = lax.axis_size("loc") == 16 and noise.shape[2] == 16 and noise.shape[1] % 3 == 0
    if sixteen and noise.shape[0] == 2 and loc_factor.shape == (HALF, 1024):
        return shards_sixteen(noise, loc_factor, *rest)
    return shards_any(noise, loc_factor, *rest)


def solution(mesh):
    placed = (
        P(None, None, ("yr", "loc"), None),
        P("loc", None),
        P(),
        P("yr", None, None),
        P("yr", None, None),
        P(),
    )
    return jax.shard_map(
        shards,
        mesh=mesh,
        in_specs=placed,
        out_specs=(P(None, None, "loc", "yr"), P(None, "loc", "yr"), P(None, "loc", "yr")),
        check_vma=False,
    )
```

```python
import functools

import jax
import jax.numpy as jnp
from jax import lax
from jax.experimental import pallas as pl
from jax.experimental.pallas import tpu as pltpu
from jax.sharding import PartitionSpec as P

REGIONS = 64
LANES = 128
HALF = 64
NT = (((1,), (1,)), ((), ()))
CHUNKS = ((8, 12, 4, 0), (9, 13, 5, 1), (10, 14, 6, 2), (11, 15, 7, 3))
FAR = (8, 12, 9, 13, 10, 14, 11, 15)
NEAR = (4, 5, 1, 6, 2, 7, 3)
LONG = pl.CostEstimate(flops=20_000_000_000, bytes_accessed=1000, transcendentals=0)


def survival(rates):
    hazard = jnp.cumsum(rates, axis=1)
    after = jnp.exp(-hazard)
    total = 0.5 + jnp.sum(after, axis=1) - 0.5 * after[:, -1]
    return total / rates.shape[1]


def shards_any(noise, loc_factor, age_factor, mean_rate, population, region_of):
    highest = lax.Precision.HIGHEST
    spread = jnp.einsum(
        "sark,lk->sarl",
        noise,
        lax.all_gather(loc_factor, "loc", axis=0, tiled=True),
        preferred_element_type=jnp.float32,
    ).astype(jnp.bfloat16)
    mixed = jnp.einsum("ab,sbrl->sarl", age_factor, spread, preferred_element_type=jnp.float32)
    log_section = (mean_rate[:, :, None, :] + mixed).astype(jnp.bfloat16)
    rates = jnp.exp(log_section.astype(jnp.float32))
    onehot = (region_of == jnp.arange(REGIONS, dtype=jnp.int32)[None, :]).astype(jnp.float32)
    totals = jnp.einsum("sal,lg->sag", population, onehot, precision=highest)
    weighted = jnp.einsum(
        "sarl,lg->sarg", population[:, :, None, :] * rates, onehot, precision=highest
    )
    region_section = survival(weighted / totals[:, :, None, :])
    region_moved = lax.all_to_all(region_section, "loc", split_axis=2, concat_axis=1, tiled=True)
    region_survival = jnp.transpose(region_moved, (0, 2, 1))
    turned = jnp.transpose(
        lax.all_to_all(log_section, "loc", split_axis=3, concat_axis=2, tiled=True), (0, 1, 3, 2)
    )
    loc_survival = survival(jnp.exp(turned.astype(jnp.float32)))
    return (turned, loc_survival, region_survival)


def tie(x, other):
    return lax.optimization_barrier((x, other))


def split_bf16(x):
    hi = x.astype(jnp.bfloat16)
    return hi, (x - hi.astype(jnp.float32)).astype(jnp.bfloat16)


PARTS = 4
TILE = 8


def age_mix_kernel(age_ref, *refs):
    xs, o_ref, done_ref, wide_ref = refs[:PARTS], *refs[PARTS:]
    ages = age_ref.shape[0]
    rows = ages * TILE
    step = 256

    @pl.when(jnp.logical_and(pl.program_id(0) == 0, pl.program_id(1) == 0))
    def _():
        pick = lax.broadcasted_iota(jnp.int32, (rows, ages), 0) >> 3
        pick = (pick == lax.broadcasted_iota(jnp.int32, (rows, ages), 1)).astype(jnp.bfloat16)
        tall = jnp.dot(pick, age_ref[...], preferred_element_type=jnp.float32).astype(jnp.bfloat16)
        spread = lax.broadcasted_iota(jnp.int32, (ages, rows), 1) >> 3
        spread = (spread == lax.broadcasted_iota(jnp.int32, (ages, rows), 0)).astype(jnp.bfloat16)
        for lo in range(0, rows, step):
            hi = min(lo + step, rows)
            both = jnp.dot(tall[lo:hi], spread[:, :hi], preferred_element_type=jnp.float32)
            same = (lax.broadcasted_iota(jnp.int32, both.shape, 0) & 7) == (
                lax.broadcasted_iota(jnp.int32, both.shape, 1) & 7
            )
            wide_ref[lo:hi, :hi] = jnp.where(same, both, 0.0).astype(jnp.bfloat16)

    done_ref[...] = jnp.zeros_like(done_ref)
    for part, x_ref in enumerate(xs):
        width = x_ref.shape[-1]
        x = x_ref[...].reshape(rows, width)
        for lo in range(0, rows, step):
            hi = min(lo + step, rows)
            mixed = jnp.dot(wide_ref[lo:hi, :hi], x[:hi], preferred_element_type=jnp.float32)
            o_ref[0, lo // TILE : hi // TILE, 0, :, part * width : (part + 1) * width] = (
                mixed.astype(jnp.bfloat16).reshape((hi - lo) // TILE, TILE, width)
            )


def age_mix(age_factor, noise):
    sexes, ages, rows, cols = noise.shape
    tiles = rows // TILE
    x = noise.reshape(sexes, ages, tiles, TILE, cols)
    width = cols // PARTS

    def part_spec(part):
        return pl.BlockSpec((1, ages, 1, TILE, width), lambda s, t: (s, 0, t, 0, part))

    mixed, done = pl.pallas_call(
        age_mix_kernel,
        out_shape=(
            jax.ShapeDtypeStruct(x.shape, jnp.bfloat16),
            jax.ShapeDtypeStruct((8, LANES), jnp.float32),
        ),
        grid=(sexes, tiles),
        in_specs=[pl.BlockSpec((ages, ages), lambda s, t: (0, 0))] + [part_spec(p) for p in range(PARTS)],
        out_specs=(
            pl.BlockSpec((1, ages, 1, TILE, cols), lambda s, t: (s, 0, t, 0, 0)),
            pl.BlockSpec((8, LANES), lambda s, t: (0, 0)),
        ),
        scratch_shapes=[pltpu.VMEM((ages * TILE, ages * TILE), jnp.bfloat16)],
        compiler_params=pltpu.CompilerParams(vmem_limit_bytes=57 << 20),
        cost_estimate=LONG,
        name="age_mix",
    )(age_factor, *([x] * PARTS))
    return mixed.reshape(sexes, ages * rows, cols), done


def merge_pair(pair, odd_device, swapped):
    axis = pair.ndim - 1
    turned = pltpu.roll(pair, HALF, axis)
    first = jnp.where(odd_device, turned, pair)
    second = jnp.where(odd_device, pair, turned)
    low = lax.broadcasted_iota(jnp.int32, pair.shape[:-2] + (1, LANES), axis) < HALF
    s = 1 if swapped else 0
    return jnp.where(low, first[..., s : s + 1, :], second[..., 1 - s : 2 - s, :])


def loc_mix_kernel(groups, blocks, d_ref, x_ref, *refs):
    factors, refs = refs[:blocks], refs[blocks:]
    count = 4 * len(groups)
    means, outs, done_ref = refs[:count], refs[count + 1 : 2 * count + 1], refs[2 * count + 1]
    done_ref[...] = jnp.zeros_like(done_ref)
    if blocks > len(groups):
        joined_ref = refs[2 * count + 2]
        for i, f in enumerate(factors):
            joined_ref[i * HALF : (i + 1) * HALF, :] = f[...]
        factors = (joined_ref,)
    ages, rows, _ = outs[0].shape
    low = lax.broadcasted_iota(jnp.int32, (1, LANES), 1) < HALF
    for c, bits in enumerate(groups):
        parts = [factors[c][i * HALF : (i + 1) * HALF, :] for i in range(4)]
        sums = []
        for s, order in enumerate(((0, 1, 2, 3), (1, 0, 3, 2))):
            factor = jnp.concatenate([parts[i] for i in order], 0)
            sums.append(lax.dot_general(x_ref[s], factor, NT, preferred_element_type=jnp.float32))
        for q in range(4):
            g = (q // 2) * LANES
            a, b = [x[:, g : g + LANES] for x in sums]
            v = jnp.where(low, a, b) if q % 2 == 0 else jnp.where(low, b, a)
            at = 4 * c + q
            m = merge_pair(means[at][...], ((d_ref[0] ^ bits[q]) & 1) == 1, q % 2 == 1)
            outs[at][...] = (v.reshape(ages, rows, LANES) + m).astype(jnp.bfloat16)


def loc_mix(device, groups, mixed, factors, mean_t, done):
    sexes, rows, cols = mixed.shape
    ages = mean_t.shape[0]
    steps = 3
    block = ages // steps
    per_age = rows // ages
    every = [b for bits in groups for b in bits]
    msg = pltpu.HBM((ages, per_age, LANES), jnp.bfloat16)
    flag_spec = pl.BlockSpec(done.shape, lambda i, d: (0, 0))

    def mean_spec(b):
        return pl.BlockSpec((block, sexes, LANES), lambda i, d: (i, 0, (d[0] ^ b) // 2))

    outs = [msg] * len(every) + [jax.ShapeDtypeStruct(done.shape, done.dtype)]
    out_specs = [pl.BlockSpec((block, per_age, LANES), lambda i, d: (i, 0, 0))] * len(every) + [flag_spec]
    if len(factors) > len(groups):
        outs.append(jax.ShapeDtypeStruct((4 * HALF, cols), jnp.bfloat16))
        out_specs.append(pl.BlockSpec((4 * HALF, cols), lambda i, d: (0, 0)))
    return pl.pallas_call(
        functools.partial(loc_mix_kernel, groups, len(factors)),
        out_shape=outs,
        grid_spec=pltpu.PrefetchScalarGridSpec(
            num_scalar_prefetch=1,
            grid=(steps,),
            in_specs=[pl.BlockSpec((sexes, block * per_age, cols), lambda i, d: (0, i, 0))]
            + [pl.BlockSpec(f.shape, lambda i, d: (0, 0)) for f in factors]
            + [mean_spec(b) for b in every]
            + [flag_spec],
            out_specs=out_specs,
        ),
        compiler_params=pltpu.CompilerParams(vmem_limit_bytes=57 << 20),
        cost_estimate=LONG,
        name="loc_mix",
    )(device, mixed, *factors, *([mean_t] * len(every)), done)


def survive_kernel(d_ref, *refs):
    count = 4 * len(CHUNKS)
    xs, pops, regs = refs[:count], refs[count : 2 * count], refs[2 * count : 3 * count]
    locs, region_ref, hi_ref, lo_ref, pop_ref, wsum_ref, psum_ref = refs[3 * count + 1 :]
    ages, rows, _ = xs[0].shape
    zero = jnp.zeros((rows, LANES), jnp.float32)
    lane = lax.broadcasted_iota(jnp.int32, (1, LANES), 1)
    low = lane < HALF
    for c, bits in enumerate(CHUNKS):
        dests = [d_ref[0] ^ b for b in bits]
        odd = [(e & 1) == 1 for e in dests]
        first = 4 * c

        def age_step(a, carry):
            hazards, totals = carry
            new_h, new_t = [], []
            at = pl.ds(pl.multiple_of(a * rows, rows), rows)
            for q in range(4):
                lanes = slice(q * LANES, (q + 1) * LANES)
                rate = jnp.exp(xs[first + q][a].astype(jnp.float32))
                h = hazards[q] + rate
                new_h.append(h)
                new_t.append(totals[q] + jnp.exp(-h))
                pop = merge_pair(pops[first + q][a], odd[q], q % 2 == 1)
                pop_ref[q, pl.ds(a, 1), :] = pop
                hi, lo = split_bf16(rate * pop)
                hi_ref[at, lanes] = hi
                lo_ref[at, lanes] = lo
            return tuple(new_h), tuple(new_t)

        hazards, totals = lax.fori_loop(0, ages, age_step, ((zero,) * 4, (zero,) * 4), unroll=3)
        onehots = []
        for q in range(4):
            out = (totals[q] + (0.5 - 0.5 * jnp.exp(-hazards[q]))) * (1.0 / ages)
            if q % 2 == 1:
                out = pltpu.roll(out, HALF, 1)
            locs[dests[q]] = out
            pair = regs[first + q][...]
            turned = pltpu.roll(pair, HALF, 1)
            mine = jnp.where(low, jnp.where(odd[q], turned, pair), jnp.where(odd[q], pair, turned))
            upper = low if q % 2 == 1 else jnp.logical_not(low)
            target = mine + jnp.where(upper, REGIONS, 0)
            region = lax.broadcasted_iota(jnp.int32, (LANES, LANES), 0)
            onehots.append(jnp.where(region == target, 1.0, 0.0).astype(jnp.bfloat16))
        onehot = jnp.concatenate(onehots, 1)

        def regions(x):
            return lax.dot_general(x, onehot, NT, preferred_element_type=jnp.float32)

        pop_hi, pop_lo = split_bf16(jnp.concatenate([pop_ref[q] for q in range(4)], 1))
        wsum = regions(hi_ref[...]) + regions(lo_ref[...])
        psum = regions(pop_hi) + regions(pop_lo)
        if c > 0:
            wsum = wsum + wsum_ref[...]
            psum = psum + psum_ref[...]
        wsum_ref[...] = wsum
        psum_ref[...] = psum

    def region_step(a, carry):
        h, t = carry
        at = pl.ds(pl.multiple_of(a * rows, rows), rows)
        h = h + wsum_ref[at, :] / psum_ref[pl.ds(a, 1), :]
        return h, t + jnp.exp(-h)

    h, t = lax.fori_loop(0, ages, region_step, (zero, zero), unroll=3)
    region_ref[...] = (t + (0.5 - 0.5 * jnp.exp(-h))) * (1.0 / ages)


def survive(device, sent, pop_t, region_row, done):
    every = [b for bits in CHUNKS for b in bits]
    ages, rows, _ = sent[0].shape
    sexes, locs = pop_t.shape[1], pop_t.shape[2] // HALF
    f32 = jnp.float32
    whole = lambda *shape: pl.BlockSpec(shape, lambda i, d: (0,) * len(shape))

    def pop_spec(b):
        return pl.BlockSpec((ages, sexes, LANES), lambda i, d: (0, 0, (d[0] ^ b) // 2))

    def region_spec(b):
        return pl.BlockSpec((1, LANES), lambda i, d: (0, (d[0] ^ b) // 2))

    return pl.pallas_call(
        survive_kernel,
        out_shape=(
            jax.ShapeDtypeStruct((locs, rows, LANES), f32),
            jax.ShapeDtypeStruct((rows, LANES), f32),
        ),
        grid_spec=pltpu.PrefetchScalarGridSpec(
            num_scalar_prefetch=1,
            grid=(1,),
            in_specs=[whole(ages, rows, LANES)] * len(every)
            + [pop_spec(b) for b in every]
            + [region_spec(b) for b in every]
            + [whole(*done.shape)],
            out_specs=(whole(locs, rows, LANES), whole(rows, LANES)),
            scratch_shapes=[
                pltpu.VMEM((ages * rows, 4 * LANES), jnp.bfloat16),
                pltpu.VMEM((ages * rows, 4 * LANES), jnp.bfloat16),
                pltpu.VMEM((4, ages, LANES), f32),
                pltpu.VMEM((ages * rows, LANES), f32),
                pltpu.VMEM((ages, LANES), f32),
            ],
        ),
        compiler_params=pltpu.CompilerParams(vmem_limit_bytes=57 << 20),
        cost_estimate=LONG,
        name="survive",
    )(device, *[sent[b] for b in every], *([pop_t] * len(every)), *([region_row] * len(every)), done)


def turn_kernel(near, d_ref, *refs):
    xs, out_ref, order_ref = refs[:8], refs[-2], refs[-1]
    d = d_ref[0]
    ages = xs[0].shape[0]
    for m in range(8):
        order_ref[(d & 7) ^ m] = xs[m][...]
    upper = (lax.broadcasted_iota(jnp.int32, (HALF, LANES), 1) >= HALF).astype(jnp.int32)
    swapped = (upper ^ ((d >> 2) & 1) ^ (1 if near else 0)) == 1
    for a in range(ages):
        tile = order_ref[:, a].reshape(LANES, LANES)
        t = tile.T.astype(jnp.float32)
        top, bottom = t[:HALF], t[HALF:]
        out_ref[0, a] = jnp.where(swapped, bottom, top).astype(jnp.bfloat16)
        out_ref[1, a] = jnp.where(swapped, top, bottom).astype(jnp.bfloat16)


def turn(device, messages, out_shape, previous, ready=()):
    near = previous is None
    ages, rows, _ = messages[0].shape
    steps = 3
    block = ages // steps
    in_specs = [pl.BlockSpec((block, rows, LANES), lambda i, d: (i, 0, 0))] * 8
    args = list(messages)
    flip = 0 if near else 1
    aliases = {}
    if not near:
        in_specs += [pl.BlockSpec(memory_space=pl.ANY)] * (1 + len(ready))
        args += [previous, *ready]
        aliases = {9: 0}
    return pl.pallas_call(
        functools.partial(turn_kernel, near),
        out_shape=out_shape,
        grid_spec=pltpu.PrefetchScalarGridSpec(
            num_scalar_prefetch=1,
            grid=(steps,),
            in_specs=in_specs,
            out_specs=pl.BlockSpec((2, block, HALF, LANES), lambda i, d: (0, i, 0, (d[0] // 8) ^ flip)),
            scratch_shapes=[pltpu.VMEM((8, block, rows, LANES), jnp.bfloat16)],
        ),
        input_output_aliases=aliases,
        compiler_params=pltpu.CompilerParams(vmem_limit_bytes=(57 if near else 24) << 20),
        cost_estimate=LONG,
        name="turn",
    )(device, *args)


def exchange(by_device, region_part, sexes):
    devices, rows, _ = by_device.shape
    mine = REGIONS // devices
    region_out = region_part.reshape(rows, sexes, devices, mine)
    region_out = jnp.transpose(region_out, (2, 1, 3, 0)).reshape(devices, 1, sexes * mine * rows)
    packed = jnp.concatenate([by_device, region_out], axis=1)
    return lax.all_to_all(packed, "loc", split_axis=0, concat_axis=0, tiled=True)


def unpack(small, rows, sexes):
    devices = small.shape[0]
    mine = REGIONS // devices
    loc_survival = jnp.transpose(small[:, :rows].reshape(devices * rows, LANES), (1, 0))
    region_survival = jnp.transpose(
        small[:, rows].reshape(devices, sexes, mine, rows), (1, 2, 0, 3)
    ).reshape(sexes, mine, devices * rows)
    return loc_survival.reshape(sexes, HALF, devices * rows), region_survival


def shards_sixteen(noise, loc_factor, age_factor, mean_rate, population, region_of):
    sexes, ages, rows, locs = noise.shape
    devices = lax.axis_size("loc")
    here = lax.axis_index("loc")

    def swap(x, bits):
        return lax.ppermute(x, "loc", [(i, i ^ bits) for i in range(devices)])

    mean_t = jnp.transpose(mean_rate, (1, 0, 2))
    pop_t = jnp.transpose(population, (1, 0, 2))
    region_row = region_of.reshape(1, locs)
    device = here[None]

    factors = {0: loc_factor}
    for bits in (8, 12, 4):
        factors[bits] = swap(loc_factor, bits)
    mixed, done = age_mix(age_factor, noise)
    factors, done = tie(factors, done)

    sent = {}

    def mix(groups, lanes, done):
        out = loc_mix(device, groups, mixed, lanes, mean_t, done)
        count = 4 * len(groups)
        sent.update(zip([b for bits in groups for b in bits], out[:count]))
        return out[count:]

    done, lane0 = mix(CHUNKS[:1], [factors[b] for b in CHUNKS[0]], done)
    lanes = [swap(lane0, bits) for bits in (1, 2, 3)]
    (done,) = mix(CHUNKS[1:2], lanes[:1], done)
    lanes, done = tie(lanes, done)
    (done,) = mix(CHUNKS[2:], lanes[1:], done)

    got = {0: sent[0]}
    for i, b in enumerate(NEAR):
        message = sent[b]
        if 0 < i < 3:
            message, done = tie(message, done)
        if i >= 2:
            message, got[NEAR[i - 2]] = tie(message, got[NEAR[i - 2]])
        got[b] = swap(message, b)
    sums = None
    for i, b in enumerate(FAR):
        message = sent[b]
        if i >= 2:
            ahead = FAR[max(i - 3, min(i - 2, 1))]
            message, got[ahead] = tie(message, got[ahead])
        if i == 5:
            sums = survive(device, sent, pop_t, region_row, done)
            small = exchange(*sums, sexes)
            message, small = tie(message, small)
        got[b] = swap(message, b)

    shape = jax.ShapeDtypeStruct((sexes, ages, HALF, devices * rows), jnp.bfloat16)
    close = [got[b] for b in range(8)]
    half = turn(device, close, shape, None)
    loc_survival, region_survival = unpack(small, rows, sexes)
    ready = (loc_survival, region_survival)
    log_rates = turn(device, [got[b] for b in range(8, 16)], shape, half, ready)
    return (log_rates, loc_survival, region_survival)


def shards(noise, loc_factor, *rest):
    sixteen = lax.axis_size("loc") == 16 and noise.shape[2] == 16 and noise.shape[1] % 3 == 0
    if sixteen and noise.shape[0] == 2 and loc_factor.shape == (HALF, 1024):
        return shards_sixteen(noise, loc_factor, *rest)
    return shards_any(noise, loc_factor, *rest)


def solution(mesh):
    placed = (
        P(None, None, ("yr", "loc"), None),
        P("loc", None),
        P(),
        P("yr", None, None),
        P("yr", None, None),
        P(),
    )
    return jax.shard_map(
        shards,
        mesh=mesh,
        in_specs=placed,
        out_specs=(P(None, None, "loc", "yr"), P(None, "loc", "yr"), P(None, "loc", "yr")),
        check_vma=False,
    )
```

```python
import functools

import jax
import jax.numpy as jnp
from jax import lax
from jax.experimental import pallas as pl
from jax.experimental.pallas import tpu as pltpu
from jax.sharding import PartitionSpec as P

REGIONS = 64
LANES = 128
HALF = 64
NT = (((1,), (1,)), ((), ()))
CHUNKS = ((8, 12, 4, 0), (9, 13, 5, 1), (10, 14, 6, 2), (11, 15, 7, 3))
FAR = (8, 12, 9, 13, 10, 14, 11, 15)
NEAR = (4, 5, 1, 6, 2, 7, 3)
LONG = pl.CostEstimate(flops=20_000_000_000, bytes_accessed=1000, transcendentals=0)


def survival(rates):
    hazard = jnp.cumsum(rates, axis=1)
    after = jnp.exp(-hazard)
    total = 0.5 + jnp.sum(after, axis=1) - 0.5 * after[:, -1]
    return total / rates.shape[1]


def shards_any(noise, loc_factor, age_factor, mean_rate, population, region_of):
    highest = lax.Precision.HIGHEST
    spread = jnp.einsum(
        "sark,lk->sarl",
        noise,
        lax.all_gather(loc_factor, "loc", axis=0, tiled=True),
        preferred_element_type=jnp.float32,
    ).astype(jnp.bfloat16)
    mixed = jnp.einsum("ab,sbrl->sarl", age_factor, spread, preferred_element_type=jnp.float32)
    log_section = (mean_rate[:, :, None, :] + mixed).astype(jnp.bfloat16)
    rates = jnp.exp(log_section.astype(jnp.float32))
    onehot = (region_of == jnp.arange(REGIONS, dtype=jnp.int32)[None, :]).astype(jnp.float32)
    totals = jnp.einsum("sal,lg->sag", population, onehot, precision=highest)
    weighted = jnp.einsum(
        "sarl,lg->sarg", population[:, :, None, :] * rates, onehot, precision=highest
    )
    region_section = survival(weighted / totals[:, :, None, :])
    region_moved = lax.all_to_all(region_section, "loc", split_axis=2, concat_axis=1, tiled=True)
    region_survival = jnp.transpose(region_moved, (0, 2, 1))
    turned = jnp.transpose(
        lax.all_to_all(log_section, "loc", split_axis=3, concat_axis=2, tiled=True), (0, 1, 3, 2)
    )
    loc_survival = survival(jnp.exp(turned.astype(jnp.float32)))
    return (turned, loc_survival, region_survival)


def tie(x, other):
    return lax.optimization_barrier((x, other))


def split_bf16(x):
    hi = x.astype(jnp.bfloat16)
    return hi, (x - hi.astype(jnp.float32)).astype(jnp.bfloat16)


PARTS = 4
TILE = 8


def age_mix_kernel(age_ref, *refs):
    xs, o_ref, done_ref, wide_ref = refs[:PARTS], *refs[PARTS:]
    ages = age_ref.shape[0]
    rows = ages * TILE
    step = 256

    @pl.when(jnp.logical_and(pl.program_id(0) == 0, pl.program_id(1) == 0))
    def _():
        pick = lax.broadcasted_iota(jnp.int32, (rows, ages), 0) >> 3
        pick = (pick == lax.broadcasted_iota(jnp.int32, (rows, ages), 1)).astype(jnp.bfloat16)
        tall = jnp.dot(pick, age_ref[...], preferred_element_type=jnp.float32).astype(jnp.bfloat16)
        spread = lax.broadcasted_iota(jnp.int32, (ages, rows), 1) >> 3
        spread = (spread == lax.broadcasted_iota(jnp.int32, (ages, rows), 0)).astype(jnp.bfloat16)
        for lo in range(0, rows, step):
            hi = min(lo + step, rows)
            both = jnp.dot(tall[lo:hi], spread[:, :hi], preferred_element_type=jnp.float32)
            same = (lax.broadcasted_iota(jnp.int32, both.shape, 0) & 7) == (
                lax.broadcasted_iota(jnp.int32, both.shape, 1) & 7
            )
            wide_ref[lo:hi, :hi] = jnp.where(same, both, 0.0).astype(jnp.bfloat16)

    done_ref[...] = jnp.zeros_like(done_ref)
    for part, x_ref in enumerate(xs):
        width = x_ref.shape[-1]
        x = x_ref[...].reshape(rows, width)
        for lo in range(0, rows, step):
            hi = min(lo + step, rows)
            mixed = jnp.dot(wide_ref[lo:hi, :hi], x[:hi], preferred_element_type=jnp.float32)
            o_ref[0, lo // TILE : hi // TILE, 0, :, part * width : (part + 1) * width] = (
                mixed.astype(jnp.bfloat16).reshape((hi - lo) // TILE, TILE, width)
            )


def age_mix(age_factor, noise):
    sexes, ages, rows, cols = noise.shape
    tiles = rows // TILE
    x = noise.reshape(sexes, ages, tiles, TILE, cols)
    width = cols // PARTS

    def part_spec(part):
        return pl.BlockSpec((1, ages, 1, TILE, width), lambda s, t: (s, 0, t, 0, part))

    mixed, done = pl.pallas_call(
        age_mix_kernel,
        out_shape=(
            jax.ShapeDtypeStruct(x.shape, jnp.bfloat16),
            pltpu.HBM((8, LANES), jnp.float32),
        ),
        grid=(sexes, tiles),
        in_specs=[pl.BlockSpec((ages, ages), lambda s, t: (0, 0))] + [part_spec(p) for p in range(PARTS)],
        out_specs=(
            pl.BlockSpec((1, ages, 1, TILE, cols), lambda s, t: (s, 0, t, 0, 0)),
            pl.BlockSpec((8, LANES), lambda s, t: (0, 0)),
        ),
        scratch_shapes=[pltpu.VMEM((ages * TILE, ages * TILE), jnp.bfloat16)],
        compiler_params=pltpu.CompilerParams(vmem_limit_bytes=57 << 20),
        cost_estimate=LONG,
        name="age_mix",
    )(age_factor, *([x] * PARTS))
    return mixed.reshape(sexes, ages * rows, cols), done


def merge_pair(pair, odd_device, swapped):
    axis = pair.ndim - 1
    turned = pltpu.roll(pair, HALF, axis)
    first = jnp.where(odd_device, turned, pair)
    second = jnp.where(odd_device, pair, turned)
    low = lax.broadcasted_iota(jnp.int32, pair.shape[:-2] + (1, LANES), axis) < HALF
    s = 1 if swapped else 0
    return jnp.where(low, first[..., s : s + 1, :], second[..., 1 - s : 2 - s, :])


def loc_mix_kernel(groups, blocks, d_ref, x_ref, *refs):
    factors, refs = refs[:blocks], refs[blocks:]
    count = 4 * len(groups)
    means, outs, done_ref = refs[:count], refs[count + 1 : 2 * count + 1], refs[2 * count + 1]
    done_ref[...] = jnp.zeros_like(done_ref)
    if blocks > len(groups):
        joined_ref = refs[2 * count + 2]
        for i, f in enumerate(factors):
            joined_ref[i * HALF : (i + 1) * HALF, :] = f[...]
        factors = (joined_ref,)
    ages, rows, _ = outs[0].shape
    low = lax.broadcasted_iota(jnp.int32, (1, LANES), 1) < HALF
    for c, bits in enumerate(groups):
        parts = [factors[c][i * HALF : (i + 1) * HALF, :] for i in range(4)]
        sums = []
        for s, order in enumerate(((0, 1, 2, 3), (1, 0, 3, 2))):
            factor = jnp.concatenate([parts[i] for i in order], 0)
            sums.append(lax.dot_general(x_ref[s], factor, NT, preferred_element_type=jnp.float32))
        for q in range(4):
            g = (q // 2) * LANES
            a, b = [x[:, g : g + LANES] for x in sums]
            v = jnp.where(low, a, b) if q % 2 == 0 else jnp.where(low, b, a)
            at = 4 * c + q
            m = merge_pair(means[at][...], ((d_ref[0] ^ bits[q]) & 1) == 1, q % 2 == 1)
            outs[at][...] = (v.reshape(ages, rows, LANES) + m).astype(jnp.bfloat16)


def loc_mix(device, groups, mixed, factors, mean_t, done):
    sexes, rows, cols = mixed.shape
    ages = mean_t.shape[0]
    steps = 3
    block = ages // steps
    per_age = rows // ages
    every = [b for bits in groups for b in bits]
    msg = pltpu.HBM((ages, per_age, LANES), jnp.bfloat16)
    flag_spec = pl.BlockSpec(done.shape, lambda i, d: (0, 0))

    def mean_spec(b):
        return pl.BlockSpec((block, sexes, LANES), lambda i, d: (i, 0, (d[0] ^ b) // 2))

    outs = [msg] * len(every) + [pltpu.HBM(done.shape, done.dtype)]
    out_specs = [pl.BlockSpec((block, per_age, LANES), lambda i, d: (i, 0, 0))] * len(every) + [flag_spec]
    if len(factors) > len(groups):
        outs.append(jax.ShapeDtypeStruct((4 * HALF, cols), jnp.bfloat16))
        out_specs.append(pl.BlockSpec((4 * HALF, cols), lambda i, d: (0, 0)))
    return pl.pallas_call(
        functools.partial(loc_mix_kernel, groups, len(factors)),
        out_shape=outs,
        grid_spec=pltpu.PrefetchScalarGridSpec(
            num_scalar_prefetch=1,
            grid=(steps,),
            in_specs=[pl.BlockSpec((sexes, block * per_age, cols), lambda i, d: (0, i, 0))]
            + [pl.BlockSpec(f.shape, lambda i, d: (0, 0)) for f in factors]
            + [mean_spec(b) for b in every]
            + [pl.BlockSpec(memory_space=pl.ANY)],
            out_specs=out_specs,
        ),
        compiler_params=pltpu.CompilerParams(vmem_limit_bytes=(57 if len(factors) == len(groups) else 52) << 20),
        cost_estimate=LONG,
        name="loc_mix",
    )(device, mixed, *factors, *([mean_t] * len(every)), done)


def survive_kernel(d_ref, *refs):
    count = 4 * len(CHUNKS)
    xs, pops, regs = refs[:count], refs[count : 2 * count], refs[2 * count : 3 * count]
    locs, region_ref, hi_ref, lo_ref, pop_ref, wsum_ref, psum_ref = refs[3 * count + 1 :]
    ages, rows, _ = xs[0].shape
    zero = jnp.zeros((rows, LANES), jnp.float32)
    lane = lax.broadcasted_iota(jnp.int32, (1, LANES), 1)
    low = lane < HALF
    for c, bits in enumerate(CHUNKS):
        dests = [d_ref[0] ^ b for b in bits]
        odd = [(e & 1) == 1 for e in dests]
        first = 4 * c

        def age_step(a, carry):
            hazards, totals = carry
            new_h, new_t = [], []
            at = pl.ds(pl.multiple_of(a * rows, rows), rows)
            for q in range(4):
                lanes = slice(q * LANES, (q + 1) * LANES)
                rate = jnp.exp(xs[first + q][a].astype(jnp.float32))
                h = hazards[q] + rate
                new_h.append(h)
                new_t.append(totals[q] + jnp.exp(-h))
                pop = merge_pair(pops[first + q][a], odd[q], q % 2 == 1)
                pop_ref[q, pl.ds(a, 1), :] = pop
                hi, lo = split_bf16(rate * pop)
                hi_ref[at, lanes] = hi
                lo_ref[at, lanes] = lo
            return tuple(new_h), tuple(new_t)

        hazards, totals = lax.fori_loop(0, ages, age_step, ((zero,) * 4, (zero,) * 4), unroll=3)
        onehots = []
        for q in range(4):
            out = (totals[q] + (0.5 - 0.5 * jnp.exp(-hazards[q]))) * (1.0 / ages)
            if q % 2 == 1:
                out = pltpu.roll(out, HALF, 1)
            locs[dests[q]] = out
            pair = regs[first + q][...]
            turned = pltpu.roll(pair, HALF, 1)
            mine = jnp.where(low, jnp.where(odd[q], turned, pair), jnp.where(odd[q], pair, turned))
            upper = low if q % 2 == 1 else jnp.logical_not(low)
            target = mine + jnp.where(upper, REGIONS, 0)
            region = lax.broadcasted_iota(jnp.int32, (LANES, LANES), 0)
            onehots.append(jnp.where(region == target, 1.0, 0.0).astype(jnp.bfloat16))
        onehot = jnp.concatenate(onehots, 1)

        def regions(x):
            return lax.dot_general(x, onehot, NT, preferred_element_type=jnp.float32)

        pop_hi, pop_lo = split_bf16(jnp.concatenate([pop_ref[q] for q in range(4)], 1))
        wsum = regions(hi_ref[...]) + regions(lo_ref[...])
        psum = regions(pop_hi) + regions(pop_lo)
        if c > 0:
            wsum = wsum + wsum_ref[...]
            psum = psum + psum_ref[...]
        wsum_ref[...] = wsum
        psum_ref[...] = psum

    def region_step(a, carry):
        h, t = carry
        at = pl.ds(pl.multiple_of(a * rows, rows), rows)
        h = h + wsum_ref[at, :] / psum_ref[pl.ds(a, 1), :]
        return h, t + jnp.exp(-h)

    h, t = lax.fori_loop(0, ages, region_step, (zero, zero), unroll=3)
    region_ref[...] = (t + (0.5 - 0.5 * jnp.exp(-h))) * (1.0 / ages)


def survive(device, sent, pop_t, region_row, done):
    every = [b for bits in CHUNKS for b in bits]
    ages, rows, _ = sent[0].shape
    sexes, locs = pop_t.shape[1], pop_t.shape[2] // HALF
    f32 = jnp.float32
    whole = lambda *shape: pl.BlockSpec(shape, lambda i, d: (0,) * len(shape))

    def pop_spec(b):
        return pl.BlockSpec((ages, sexes, LANES), lambda i, d: (0, 0, (d[0] ^ b) // 2))

    def region_spec(b):
        return pl.BlockSpec((1, LANES), lambda i, d: (0, (d[0] ^ b) // 2))

    return pl.pallas_call(
        survive_kernel,
        out_shape=(
            jax.ShapeDtypeStruct((locs, rows, LANES), f32),
            jax.ShapeDtypeStruct((rows, LANES), f32),
        ),
        grid_spec=pltpu.PrefetchScalarGridSpec(
            num_scalar_prefetch=1,
            grid=(1,),
            in_specs=[whole(ages, rows, LANES)] * len(every)
            + [pop_spec(b) for b in every]
            + [region_spec(b) for b in every]
            + [pl.BlockSpec(memory_space=pl.ANY)],
            out_specs=(whole(locs, rows, LANES), whole(rows, LANES)),
            scratch_shapes=[
                pltpu.VMEM((ages * rows, 4 * LANES), jnp.bfloat16),
                pltpu.VMEM((ages * rows, 4 * LANES), jnp.bfloat16),
                pltpu.VMEM((4, ages, LANES), f32),
                pltpu.VMEM((ages * rows, LANES), f32),
                pltpu.VMEM((ages, LANES), f32),
            ],
        ),
        compiler_params=pltpu.CompilerParams(vmem_limit_bytes=57 << 20),
        cost_estimate=LONG,
        name="survive",
    )(device, *[sent[b] for b in every], *([pop_t] * len(every)), *([region_row] * len(every)), done)


def turn_kernel(near, d_ref, *refs):
    xs, out_ref, order_ref = refs[:8], refs[-2], refs[-1]
    d = d_ref[0]
    ages = xs[0].shape[0]
    for m in range(8):
        order_ref[(d & 7) ^ m] = xs[m][...]
    upper = (lax.broadcasted_iota(jnp.int32, (HALF, LANES), 1) >= HALF).astype(jnp.int32)
    swapped = (upper ^ ((d >> 2) & 1) ^ (1 if near else 0)) == 1
    for a in range(ages):
        tile = order_ref[:, a].reshape(LANES, LANES)
        t = tile.T.astype(jnp.float32)
        top, bottom = t[:HALF], t[HALF:]
        out_ref[0, a] = jnp.where(swapped, bottom, top).astype(jnp.bfloat16)
        out_ref[1, a] = jnp.where(swapped, top, bottom).astype(jnp.bfloat16)


def turn(device, messages, out_shape, previous, ready=()):
    near = previous is None
    ages, rows, _ = messages[0].shape
    steps = 3
    block = ages // steps
    in_specs = [pl.BlockSpec((block, rows, LANES), lambda i, d: (i, 0, 0))] * 8
    args = list(messages)
    flip = 0 if near else 1
    aliases = {}
    if not near:
        in_specs += [pl.BlockSpec(memory_space=pl.ANY)] * (1 + len(ready))
        args += [previous, *ready]
        aliases = {9: 0}
    return pl.pallas_call(
        functools.partial(turn_kernel, near),
        out_shape=out_shape,
        grid_spec=pltpu.PrefetchScalarGridSpec(
            num_scalar_prefetch=1,
            grid=(steps,),
            in_specs=in_specs,
            out_specs=pl.BlockSpec((2, block, HALF, LANES), lambda i, d: (0, i, 0, (d[0] // 8) ^ flip)),
            scratch_shapes=[pltpu.VMEM((8, block, rows, LANES), jnp.bfloat16)],
        ),
        input_output_aliases=aliases,
        compiler_params=pltpu.CompilerParams(vmem_limit_bytes=(57 if near else 24) << 20),
        cost_estimate=LONG,
        name="turn",
    )(device, *args)


def exchange(by_device, region_part, sexes):
    devices, rows, _ = by_device.shape
    mine = REGIONS // devices
    region_out = region_part.reshape(rows, sexes, devices, mine)
    region_out = jnp.transpose(region_out, (2, 1, 3, 0)).reshape(devices, 1, sexes * mine * rows)
    packed = jnp.concatenate([by_device, region_out], axis=1)
    return lax.all_to_all(packed, "loc", split_axis=0, concat_axis=0, tiled=True)


def unpack(small, rows, sexes):
    devices = small.shape[0]
    mine = REGIONS // devices
    loc_survival = jnp.transpose(small[:, :rows].reshape(devices * rows, LANES), (1, 0))
    region_survival = jnp.transpose(
        small[:, rows].reshape(devices, sexes, mine, rows), (1, 2, 0, 3)
    ).reshape(sexes, mine, devices * rows)
    return loc_survival.reshape(sexes, HALF, devices * rows), region_survival


def shards_sixteen(noise, loc_factor, age_factor, mean_rate, population, region_of):
    sexes, ages, rows, locs = noise.shape
    devices = lax.axis_size("loc")
    here = lax.axis_index("loc")

    def swap(x, bits):
        return lax.ppermute(x, "loc", [(i, i ^ bits) for i in range(devices)])

    mean_t = jnp.transpose(mean_rate, (1, 0, 2))
    pop_t = jnp.transpose(population, (1, 0, 2))
    region_row = region_of.reshape(1, locs)
    device = here[None]

    factors = {0: loc_factor}
    for bits in (8, 12, 4):
        factors[bits] = swap(loc_factor, bits)
    mixed, done = age_mix(age_factor, noise)
    factors, done = tie(factors, done)

    sent = {}

    def mix(groups, lanes, done):
        out = loc_mix(device, groups, mixed, lanes, mean_t, done)
        count = 4 * len(groups)
        sent.update(zip([b for bits in groups for b in bits], out[:count]))
        return out[count:]

    done, lane0 = mix(CHUNKS[:1], [factors[b] for b in CHUNKS[0]], done)
    lanes = [swap(lane0, bits) for bits in (1, 2, 3)]
    (done,) = mix(CHUNKS[1:2], lanes[:1], done)
    lanes, done = tie(lanes, done)
    (done,) = mix(CHUNKS[2:], lanes[1:], done)

    got = {0: sent[0]}
    for i, b in enumerate(NEAR):
        message = sent[b]
        if 0 < i < 3:
            message, done = tie(message, done)
        if i >= 2:
            message, got[NEAR[i - 2]] = tie(message, got[NEAR[i - 2]])
        got[b] = swap(message, b)
    sums = None
    for i, b in enumerate(FAR):
        message = sent[b]
        if i >= 2:
            ahead = FAR[max(i - 3, min(i - 2, 1))]
            message, got[ahead] = tie(message, got[ahead])
        if i == 5:
            sums = survive(device, sent, pop_t, region_row, done)
            small = exchange(*sums, sexes)
            message, small = tie(message, small)
        got[b] = swap(message, b)

    shape = jax.ShapeDtypeStruct((sexes, ages, HALF, devices * rows), jnp.bfloat16)
    close = [got[b] for b in range(8)]
    half = turn(device, close, shape, None)
    loc_survival, region_survival = unpack(small, rows, sexes)
    ready = (loc_survival, region_survival)
    log_rates = turn(device, [got[b] for b in range(8, 16)], shape, half, ready)
    return (log_rates, loc_survival, region_survival)


def shards(noise, loc_factor, *rest):
    sixteen = lax.axis_size("loc") == 16 and noise.shape[2] == 16 and noise.shape[1] % 3 == 0
    if sixteen and noise.shape[0] == 2 and loc_factor.shape == (HALF, 1024):
        return shards_sixteen(noise, loc_factor, *rest)
    return shards_any(noise, loc_factor, *rest)


def solution(mesh):
    placed = (
        P(None, None, ("yr", "loc"), None),
        P("loc", None),
        P(),
        P("yr", None, None),
        P("yr", None, None),
        P(),
    )
    return jax.shard_map(
        shards,
        mesh=mesh,
        in_specs=placed,
        out_specs=(P(None, None, "loc", "yr"), P(None, "loc", "yr"), P(None, "loc", "yr")),
        check_vma=False,
    )
```
